32 devices in a mesh: req: 4 (over x, core), exp: 8 (over z, y).
Axes of the slice: x: 2, y: 2, z: 4, core: 2. Of those that a mesh axis runs over, the one named last changes fastest.
Arguments:
- query: bfloat16 [2048, 2048], P(('req', 'exp'))
- new_kv: bfloat16 [2048, 1024], P(('req', 'exp')), may hold values from -6 to 6
- cache_kv: bfloat16 [4, 2048, 1024], P('req', 'exp')
- cached_len: int32 [4], replicated, may hold values from 0 to 2048, as said below
- residual: bfloat16 [2048, 2048], P(('req', 'exp')), may hold values from -6 to 6
- w_out: bfloat16 [2048, 2048], replicated, may hold values from -4 to 4
- gain: float32 [2048], replicated, may hold values from 0.1 to 1.9
- routes: int32 [2048, 6], P(('req', 'exp')), may hold values from 0 to 63, all different within a row; in each aligned block of 64 rows (0 to 63, 64 to 127, ...) at most 7 rows name the same one
- gates: bfloat16 [2048, 6], P(('req', 'exp')), may hold values from 0.049804688 to 0.59765625
- w_gate: bfloat16 [128, 2048, 704], P(('req', 'exp')), may hold values from -0.125 to 0.125
- w_up: bfloat16 [128, 2048, 704], P(('req', 'exp')), may hold values from -0.125 to 0.125
- w_down: bfloat16 [128, 704, 2048], P(('req', 'exp')), may hold values from -0.3125 to 0.3125
Outputs:
- output: bfloat16 [2048, 2048], P(('req', 'exp'))
The draws below stay inside these ranges and needn't reach their ends.
Inputs may be any that keep to these rules, and one draw needn't show every extreme that they name: `routes`: in the 64 rows of one device no expert is named by more than 7 rows, a bound that some block reaches; a row names 6 different experts. `cached_len`: the largest is exactly 2048, and 1 requests have none.
All inputs are finite; a program needn't handle non-finite values.
Results may differ from the reference program's by a relative error of at most 0.033.
Values may be sent and summed in bfloat16 or wider, within the bound.
A program may use at most 128 MiB of HBM per device.

```python
import math
import jax
import jax.numpy as jnp
import numpy as np
from jax import lax

D = 2048
H = 16
KVH = 4
HD = 128
EXPERTS = 64
FF = 1408
TOPK = 6
HALVES = 2
TOK_DEV = 64
TOKENS = 2048
REQUESTS = 4
NEW = 512
CACHE = 2048
CAP = 7


def lengths_of(key):
    base = jax.random.fold_in(key, 11)
    order = jax.random.permutation(jax.random.fold_in(base, 1), REQUESTS).astype(jnp.int32)
    drawn = jax.random.randint(jax.random.fold_in(base, 2), (REQUESTS,), 1, CACHE + 1).astype(jnp.int32)
    rank = jnp.zeros((REQUESTS,), jnp.int32).at[order].set(jnp.arange(REQUESTS, dtype=jnp.int32))
    lengths = jnp.where(rank == 0, CACHE, jnp.where(rank <= REQUESTS // 3, 0, drawn))
    return lengths.astype(jnp.int32)


def cache_of(key):
    inner = jax.random.fold_in(key, 12)
    shape = (REQUESTS, CACHE, 2 * KVH * HD)
    return jax.random.normal(inner, shape, jnp.float32)


def draw_cache_kv(key, part):
    return cache_of(key).astype(jnp.bfloat16)


def draw_cached_len(key, part):
    return lengths_of(key)


def draw_query(key, part):
    base = jax.random.normal(jax.random.fold_in(key, 13), (TOKENS, H * HD), jnp.float32) * 1.5
    return base.astype(jnp.bfloat16)


def shard_levels(rng, dims, split, least, top_value):
    loudness, own = 1.0, jax.random.fold_in(rng, 6)
    for position, blocks in split:
        steps = jnp.exp(jax.random.uniform(jax.random.fold_in(own, position), (blocks,), jnp.float32, least / len(split), top_value / len(split)))
        loudness = loudness * jnp.repeat(steps, dims[position] // blocks).reshape([-1 if axis == position else 1 for axis in range(len(dims))])
    return loudness


def deal_out(rng, own, number, rows, amount, top, bound, slope):
    ranking = jax.random.permutation(rng, amount)
    crowded, ordinary = portions_of(amount, rows * top, bound, slope, True), portions_of(amount, rows * top, bound, slope, False)
    places = jnp.arange(amount)

    def named(tallies, rotation):
        used = int((tallies > 0).sum())
        fixed = max(1, used // 4)
        shifted = fixed + (places - fixed + rotation * (used - fixed)) % max(1, amount - fixed)
        return jnp.zeros((amount,), jnp.int32).at[ranking[jnp.where(places < fixed, places, shifted)]].set(jnp.asarray(tallies, jnp.int32))

    tallies = jnp.where(number % 4 == 0, named(crowded, number // 4), named(ordinary, number - number // 4 - 1))
    mixed = jax.random.permutation(jax.random.fold_in(own, 3), amount)
    giver, taker = mixed[0:amount // 2 * 2:2], mixed[1:amount // 2 * 2:2]
    room = jnp.minimum(tallies[giver] - 1, bound - tallies[taker]) // 2
    room = jnp.where((giver == ranking[0]) | (taker == ranking[0]) | (tallies[taker] == 0), 0, jnp.maximum(room, 0))
    shifted = jax.random.randint(jax.random.fold_in(own, 4), (amount // 2,), 0, 1 << 20) % (room + 1)
    tallies = tallies.at[giver].add(-shifted).at[taker].add(shifted)
    members = jnp.searchsorted(jnp.cumsum(tallies), jnp.arange(rows * top), side="right").astype(jnp.int32)
    listing = members.reshape(top, rows).T
    listing = listing[jax.random.permutation(jax.random.fold_in(own, 1), rows)]
    rotation = jax.random.randint(jax.random.fold_in(own, 2), (rows, 1), 0, top)
    return jnp.take_along_axis(listing, (jnp.arange(top)[None, :] + rotation) % top, axis=1)


def portions_of(amount, total, most, lean, full):
    weights = [(1 << 20) // math.isqrt(standing ** lean) + 1 for standing in range(1, amount + 1)]
    largest = most if full else min(most, max(-(-total // amount), total * weights[0] // sum(weights)))
    least = 1 if total - largest >= amount - 1 else 0
    holding, rest = [largest] + [least] * (amount - 1), total - largest - least * (amount - 1)
    while rest > 0:
        movable = [i for i in range(1, amount) if holding[i] < largest] or [i for i in range(1, amount) if holding[i] < most]
        pool, budget = sum([weights[i] for i in movable]), rest
        for i in movable:
            addition = min(most - holding[i], max(1, budget * weights[i] // pool), rest)
            holding[i] = holding[i] + addition
            rest = rest - addition
    return np.array(holding)


def bell_draw(stream_key, extent, width, bound, split=(), kind=jnp.bfloat16):
    values = jax.random.normal(stream_key, extent, jnp.float32) * width
    if len(split) > 0:
        values = shard_levels(stream_key, extent, split, -0.22, 0.18) * values
    return jnp.clip(values, min=-bound, max=bound).astype(kind)


def setup_inputs(seed: int = 0) -> dict:
    arg_keys = jax.random.split(jax.random.key(seed), 13)
    query = draw_query(jax.random.fold_in(arg_keys[12], 71), 0)
    new_kv = bell_draw(arg_keys[1], (TOKENS, 2 * KVH * HD), 1.0, 6.0, ((0, 32),))
    cache_kv = draw_cache_kv(jax.random.fold_in(arg_keys[12], 71), 0)
    cached_len = draw_cached_len(jax.random.fold_in(arg_keys[12], 71), 0)
    residual = bell_draw(arg_keys[4], (TOKENS, D), 1.0, 6.0, ((0, 32),))
    w_out = bell_draw(arg_keys[5], (H * HD, D), 0.3, 4.0)
    gain = jnp.clip(1.0 + 0.18 * jax.random.normal(arg_keys[6], (D,), jnp.float32), 0.1, 1.9)
    routes_keys = jax.random.split(jax.random.fold_in(arg_keys[7], 1), TOKENS // TOK_DEV)
    routes_turns = jax.random.permutation(jax.random.fold_in(arg_keys[7], 3), TOKENS // TOK_DEV)
    routes = jax.vmap(lambda own, number: deal_out(jax.random.fold_in(arg_keys[7], 2), own, number, TOK_DEV, EXPERTS, TOPK, CAP, 2))(routes_keys, routes_turns).reshape((TOKENS, TOPK))
    gates = jnp.clip(0.049804688 + 0.54785156 * jax.random.uniform(arg_keys[8], (TOKENS, TOPK), jnp.float32) ** shard_levels(arg_keys[8], (TOKENS, TOPK), ((0, 32),), -0.2, 0.2), 0.049804688, 0.59765625).astype(jnp.bfloat16)
    w_gate = bell_draw(arg_keys[9], (HALVES * EXPERTS, D, FF // HALVES), D ** -0.5, 0.125, ((0, 32),))
    w_up = bell_draw(arg_keys[10], (HALVES * EXPERTS, D, FF // HALVES), D ** -0.5, 0.125, ((0, 32),))
    w_down = bell_draw(arg_keys[11], (HALVES * EXPERTS, FF // HALVES, D), (FF // 4) ** -0.5, 0.3125, ((0, 32),))
    return {"query": query, "new_kv": new_kv, "cache_kv": cache_kv, "cached_len": cached_len, "residual": residual, "w_out": w_out, "gain": gain, "routes": routes, "gates": gates, "w_gate": w_gate, "w_up": w_up, "w_down": w_down}


def reference(query, new_kv, cache_kv, cached_len, residual, w_out, gain, routes, gates, w_gate, w_up, w_down):
    group = H // KVH
    kv_cols = KVH * HD

    def attend(items):
        queries, fresh, cached, length = items
        keys = jnp.concatenate([cached[:, :kv_cols], fresh[:, :kv_cols]], 0)
        values = jnp.concatenate([cached[:, kv_cols:], fresh[:, kv_cols:]], 0)
        qh = queries.reshape(NEW, KVH, group, HD).astype(jnp.float32)
        kh = keys.reshape(CACHE + NEW, KVH, HD).astype(jnp.float32)
        vh = values.reshape(CACHE + NEW, KVH, HD).astype(jnp.float32)
        scores = jnp.einsum('qgjd,kgd->qgjk', qh, kh) * (1.0 / math.sqrt(HD))
        place = jnp.arange(CACHE + NEW, dtype=jnp.int32)
        qplace = jnp.arange(NEW, dtype=jnp.int32)
        seen = jnp.where(place[None, :] < CACHE, place[None, :] < length, place[None, :] - CACHE <= qplace[:, None])
        masked = jnp.where(seen[:, None, None, :], scores, -1e+30)
        peak = lax.optimization_barrier(jnp.max(masked, axis=-1, keepdims=True))
        expo = jnp.where(seen[:, None, None, :], jnp.exp(masked - peak), 0.0)
        total = lax.optimization_barrier(jnp.sum(expo, axis=-1))
        weights = lax.optimization_barrier(expo.astype(jnp.bfloat16)).astype(jnp.float32)
        out = jnp.einsum('qgjk,kgd->qgjd', weights, vh) / total[..., None]
        return out.reshape(NEW, H * HD).astype(jnp.bfloat16)
    attended = lax.map(attend, (query.reshape(REQUESTS, NEW, H * HD), new_kv.reshape(REQUESTS, NEW, 2 * kv_cols), cache_kv, cached_len))
    attended = attended.reshape(TOKENS, H * HD)
    stream = (residual.astype(jnp.float32) + jnp.dot(attended, w_out, preferred_element_type=jnp.float32)).astype(jnp.bfloat16)
    wide = stream.astype(jnp.float32)
    normed = (wide * lax.rsqrt(lax.optimization_barrier(jnp.mean(wide * wide, axis=-1, keepdims=True)) + 1e-06) * gain).astype(jnp.bfloat16)
    blocks = TOKENS // TOK_DEV
    pairs = routes.reshape(blocks, TOK_DEV * TOPK)
    hits = (pairs[..., None] == jnp.arange(EXPERTS, dtype=jnp.int32)[None, None, :]).astype(jnp.int32)
    slot = lax.optimization_barrier(jnp.sum(hits * (jnp.cumsum(hits, axis=1) - 1), axis=-1))
    row = (jnp.arange(blocks, dtype=jnp.int32)[:, None] * CAP + slot).reshape(TOKENS, TOPK).astype(jnp.int32)
    source = jnp.broadcast_to(normed[:, None, :], (TOKENS, TOPK, D))
    buffer = jnp.zeros((EXPERTS, blocks * CAP, D), jnp.bfloat16).at[routes, row].set(source)

    def expert(items):
        rows_in, index = items
        summed = jnp.zeros((blocks * CAP, D), jnp.float32)
        for half in range(HALVES):
            where = (half * EXPERTS + index).astype(jnp.int32)
            gate_w = lax.dynamic_index_in_dim(w_gate, where, 0, keepdims=False)
            up_w = lax.dynamic_index_in_dim(w_up, where, 0, keepdims=False)
            down_w = lax.dynamic_index_in_dim(w_down, where, 0, keepdims=False)
            gate_v = jnp.dot(rows_in, gate_w, preferred_element_type=jnp.float32)
            up_v = jnp.dot(rows_in, up_w, preferred_element_type=jnp.float32)
            hidden = (jax.nn.silu(gate_v) * up_v).astype(jnp.bfloat16)
            part = jnp.dot(hidden, down_w, preferred_element_type=jnp.float32)
            part = lax.optimization_barrier(part.astype(jnp.bfloat16)).astype(jnp.float32)
            summed = summed + part
        return summed.astype(jnp.bfloat16)
    outs = lax.map(expert, (buffer, jnp.arange(EXPERTS, dtype=jnp.int32)))
    picked = outs[routes, row]
    mixed = jnp.einsum('tk,tkd->td', gates.astype(jnp.float32), picked.astype(jnp.float32))
    return (stream.astype(jnp.float32) + mixed).astype(jnp.bfloat16)
```

```python
import math

import jax
import jax.numpy as jnp
from jax import lax
from jax.experimental import pallas as pl
from jax.experimental.pallas import tpu as pltpu
from jax.sharding import PartitionSpec as P

D = 2048
H = 16
KVH = 4
HD = 128
EXPERTS = 64
TOPK = 6
HALVES = 2
CAP = 7


def visibility(key_row, key_device, query_index, lens_group, piece_len, tok_rows, new_len):
    req_here = lens_group.shape[0]
    cache_rows = req_here * piece_len
    is_cache = key_row < cache_rows
    cache_req = key_row // piece_len
    cache_pos = key_device * piece_len + key_row % piece_len
    new_token = key_device * tok_rows + key_row - cache_rows
    key_req = jnp.where(is_cache, cache_req, new_token // new_len)
    key_pos = new_token % new_len
    owners = jnp.arange(req_here, dtype=jnp.int32)
    cache_len = jnp.sum(
        jnp.where(cache_req[:, None] == owners[None, :], lens_group[None, :], 0), axis=1
    )
    query_req = query_index // new_len
    query_pos = query_index % new_len
    same = key_req[None, :] == query_req[:, None]
    seen = jnp.where(
        is_cache[None, :], (cache_pos < cache_len)[None, :], key_pos[None, :] <= query_pos[:, None]
    )
    return same & seen


def head_scores(queries, keys):
    count = queries.shape[0]
    qh = queries.reshape(count, KVH, H // KVH, HD)
    kh = keys.reshape(keys.shape[0], KVH, HD)
    return jnp.einsum("qgjd,kgd->qgjk", qh, kh, preferred_element_type=jnp.float32) * (
        1.0 / math.sqrt(HD)
    )


def weighted_values(weights, values):
    vh = values.reshape(values.shape[0], KVH, HD)
    return jnp.einsum("qgjk,kgd->qgjd", weights, vh, preferred_element_type=jnp.float32)


MESH = pl.DeviceIdType.MESH
VMEM_SPEC = pl.BlockSpec(memory_space=pltpu.VMEM)
ANY_SPEC = pl.BlockSpec(memory_space=pl.ANY)
OFFSETS = (1, 3, 2)


def place_here():
    row, col = lax.axis_index("req"), lax.axis_index("exp")
    return row // 2, col % 2, col // 2, row % 2


def peer(x, y, z, c):
    return (2 * x + c, 2 * z + y)


def block_of(x, y, z, c):
    return (2 * x + c) * 8 + 2 * z + y


def stepped(x, y, c, da, db):
    dx = jnp.where(c == 0, db, da)
    dy = jnp.where(c == 0, da, db)
    return jnp.bitwise_xor(x, dx), jnp.bitwise_xor(y, dy)


def greet(peers):
    barrier = pltpu.get_barrier_semaphore()
    for other in peers:
        pl.semaphore_signal(barrier, inc=1, device_id=other, device_id_type=MESH)
    pl.semaphore_wait(barrier, len(peers))


def partners(x, y, z, c):
    xa, ya = stepped(x, y, c, 1, 0)
    xb, yb = stepped(x, y, c, 0, 1)
    along = {k: peer(x, y, (z + k) % 4, c) for k in OFFSETS}
    return along, peer(xa, ya, z, c), peer(xb, yb, z, c), peer(x, y, z, 1 - c)


def label(da, db, k):
    return (da * 2 + db) * 4 + k


def gather_kernel(mine_ref, out_ref, local_sem, send_sem, recv_sem):
    x, y, z, c = place_here()
    along, a_peer, b_peer, core_peer = partners(x, y, z, c)
    greet([*along.values(), a_peer, b_peer, core_peer])
    sent = []

    def send(src, block, slot, target):
        copy = pltpu.make_async_remote_copy(
            src_ref=src,
            dst_ref=out_ref.at[block],
            send_sem=send_sem.at[len(sent)],
            recv_sem=recv_sem.at[slot],
            device_id=target,
            device_id_type=MESH,
        )
        copy.start()
        sent.append(copy)

    def arrived(block, slot):
        pltpu.make_async_remote_copy(
            src_ref=mine_ref,
            dst_ref=out_ref.at[block],
            send_sem=send_sem.at[0],
            recv_sem=recv_sem.at[slot],
            device_id=core_peer,
            device_id_type=MESH,
        ).wait_recv()

    def block(da, db, k):
        xs, ys = stepped(x, y, c, da, db)
        return block_of(xs, ys, (z + k) % 4, c)

    own = block_of(x, y, z, c)
    send(mine_ref, own, label(0, 1, 0), b_peer)
    send(mine_ref, own, label(1, 0, 0), a_peer)
    for k in OFFSETS:
        send(mine_ref, own, label(0, 0, (4 - k) % 4), along[k])
    send(mine_ref, own, 16 + label(0, 0, 0), core_peer)
    keep = pltpu.make_async_copy(mine_ref, out_ref.at[own], local_sem)
    keep.start()

    def relay(da, db, k):
        b = block(da, db, k)
        arrived(b, label(da, db, k))
        if db == 0:
            send(out_ref.at[b], b, label(da, 1, k), b_peer)
            if da == 0:
                send(out_ref.at[b], b, label(1, 0, k), a_peer)
        send(out_ref.at[b], b, 16 + label(da, db, k), core_peer)

    relay(1, 0, 0)
    for k in OFFSETS:
        relay(0, 0, k)
    relay(0, 1, 0)
    for k in OFFSETS:
        relay(1, 0, k)
    relay(1, 1, 0)
    for k in OFFSETS:
        relay(0, 1, k)
    for k in OFFSETS:
        relay(1, 1, k)
    for da in range(2):
        for db in range(2):
            for k in range(4):
                xs, ys = stepped(x, y, 1 - c, da, db)
                arrived(block_of(xs, ys, (z + k) % 4, 1 - c), 16 + label(da, db, k))
    keep.wait()
    for copy in sent:
        copy.wait_send()


def gather_rows(mine):
    rows, width = mine.shape
    return pl.pallas_call(
        gather_kernel,
        out_shape=jax.ShapeDtypeStruct((32, rows, width), mine.dtype),
        in_specs=[VMEM_SPEC],
        out_specs=ANY_SPEC,
        scratch_shapes=[
            pltpu.SemaphoreType.DMA(()),
            pltpu.SemaphoreType.DMA((31,)),
            pltpu.SemaphoreType.DMA((32,)),
        ],
        compiler_params=pltpu.CompilerParams(collective_id=1, has_side_effects=True),
        name="gather_rows",
    )(mine)


def reduce_kernel(
    part_ref, stream_ref, out_ref, in_c, in_b, in_a, in_z, sum_c, sum_b, sum_a, send_sem, recv_sem
):
    x, y, z, c = place_here()
    along, a_peer, b_peer, core_peer = partners(x, y, z, c)
    greet([*along.values(), a_peer, b_peer, core_peer])
    sent = []
    f32 = jnp.float32

    def send(src, dst, slot, target):
        copy = pltpu.make_async_remote_copy(
            src_ref=src,
            dst_ref=dst,
            send_sem=send_sem.at[len(sent)],
            recv_sem=recv_sem.at[slot],
            device_id=target,
            device_id_type=MESH,
        )
        copy.start()
        sent.append(copy)

    def arrived(dst, slot):
        pltpu.make_async_remote_copy(
            src_ref=dst,
            dst_ref=dst,
            send_sem=send_sem.at[0],
            recv_sem=recv_sem.at[slot],
            device_id=core_peer,
            device_id_type=MESH,
        ).wait_recv()

    def add(dst, one, two):
        rows = dst.shape[0]

        @pl.loop(0, rows // 16)
        def _(i):
            part = pl.ds(pl.multiple_of(i * 16, 16), 16)
            dst[part, :] = (one[part, :].astype(f32) + two[part, :].astype(f32)).astype(dst.dtype)

    ks = (*OFFSETS, 0)
    order = [(da, db, k) for db in (1, 0) for da in (1, 0) for k in ks]
    for da, db, k in order:
        xs, ys = stepped(x, y, 1 - c, da, db)
        i = label(da, db, k)
        send(part_ref.at[block_of(xs, ys, (z + k) % 4, 1 - c)], in_c.at[i], i, core_peer)
    for da, db, k in order:
        i = label(da, db, k)
        xs, ys = stepped(x, y, c, da, db)
        arrived(in_c.at[i], i)
        add(sum_c.at[i], part_ref.at[block_of(xs, ys, (z + k) % 4, c)], in_c.at[i])
        if db == 1:
            send(sum_c.at[i], in_b.at[da * 4 + k], 16 + da * 4 + k, b_peer)
    for da in (1, 0):
        for k in ks:
            j = da * 4 + k
            arrived(in_b.at[j], 16 + j)
            add(sum_b.at[j], sum_c.at[label(da, 0, k)], in_b.at[j])
            if da == 1:
                send(sum_b.at[j], in_a.at[k], 24 + k, a_peer)
    for k in ks:
        arrived(in_a.at[k], 24 + k)
        add(sum_a.at[k], sum_b.at[k], in_a.at[k])
        if k:
            send(sum_a.at[k], in_z.at[4 - k], 28 + (4 - k), along[k])
    for k in OFFSETS:
        arrived(in_z.at[k], 28 + k)
    rows = out_ref.shape[0]

    @pl.loop(0, rows // 16)
    def _(i):
        part = pl.ds(pl.multiple_of(i * 16, 16), 16)
        whole = sum_a[0, part, :].astype(f32)
        for k in OFFSETS:
            whole += in_z[k, part, :].astype(f32)
        out_ref[part, :] = (stream_ref[part, :].astype(f32) + whole).astype(out_ref.dtype)

    for copy in sent:
        copy.wait_send()


def reduce_rows(part, stream):
    rows, width = stream.shape
    space = lambda n: pltpu.VMEM((n, rows, width), jnp.bfloat16)
    return pl.pallas_call(
        reduce_kernel,
        out_shape=jax.ShapeDtypeStruct(stream.shape, stream.dtype),
        in_specs=[VMEM_SPEC, VMEM_SPEC],
        out_specs=VMEM_SPEC,
        scratch_shapes=[
            space(16),
            space(8),
            space(4),
            space(4),
            space(16),
            space(8),
            space(4),
            pltpu.SemaphoreType.DMA((31,)),
            pltpu.SemaphoreType.DMA((32,)),
        ],
        compiler_params=pltpu.CompilerParams(
            collective_id=2, has_side_effects=True, vmem_limit_bytes=48 * 2**20
        ),
        name="reduce_rows",
    )(part, stream)


def expert_kernel(rows_ref, gate_ref, up_ref, down_ref, out_ref):
    groups, _, count, width = rows_ref.shape
    rows = rows_ref[...].reshape(groups * count, width)
    gate = jnp.dot(rows, gate_ref[0], preferred_element_type=jnp.float32)
    up = jnp.dot(rows, up_ref[0], preferred_element_type=jnp.float32)
    hidden = (gate / (1.0 + jnp.exp(-gate)) * up).astype(jnp.bfloat16)
    part = jnp.dot(hidden, down_ref[0], preferred_element_type=jnp.float32)
    out_ref[...] = part.astype(jnp.bfloat16).reshape(groups, 1, count, width)


def run_experts(rows, w_gate, w_up, w_down):
    groups, here, count, width = rows.shape
    ff = w_gate.shape[2]
    lot = pl.BlockSpec((groups, 1, count, width), lambda r: (0, r, 0, 0))
    return pl.pallas_call(
        expert_kernel,
        out_shape=jax.ShapeDtypeStruct(rows.shape, rows.dtype),
        grid=(here,),
        in_specs=[
            lot,
            pl.BlockSpec((1, width, ff), lambda r: (r, 0, 0)),
            pl.BlockSpec((1, width, ff), lambda r: (r, 0, 0)),
            pl.BlockSpec((1, ff, width), lambda r: (r, 0, 0)),
        ],
        out_specs=lot,
        compiler_params=pltpu.CompilerParams(vmem_limit_bytes=48 * 2**20),
        name="run_experts",
    )(rows, w_gate, w_up, w_down)


def routed(stream, normed, routes, gates, w_gate, w_up, w_down):
    tok_rows = stream.shape[0]
    rows_here = w_gate.shape[0]
    axes = ("req", "exp")
    me = lax.axis_index("req") * lax.axis_size("exp") + lax.axis_index("exp")
    flat = routes.reshape(-1)
    hits = (flat[:, None] == jnp.arange(EXPERTS, dtype=jnp.int32)[None, :]).astype(jnp.int32)
    slot = jnp.sum(hits * (jnp.cumsum(hits, axis=0) - 1), axis=1)
    place = (flat * CAP + slot).reshape(tok_rows, TOPK)
    places = lax.all_gather(place, axes, axis=0, tiled=True)
    shares = lax.all_gather(gates, axes, axis=0, tiled=True).astype(jnp.float32)
    tokens = places.shape[0]
    first = me * rows_here % EXPERTS * CAP
    rel = places - first
    lot = jnp.arange(tokens, dtype=jnp.int32)[:, None] // tok_rows % 4
    row = rel // CAP * 32 + lot * CAP + rel % CAP
    row = jnp.where((rel >= 0) & (rel < rows_here * CAP), row, -1).reshape(8, tokens // 8, TOPK)
    shares = shares.reshape(8, tokens // 8, TOPK)
    lanes = jnp.arange(rows_here * 32, dtype=jnp.int32)
    pick = jnp.zeros((8, tokens // 8, rows_here * 32), jnp.float32)
    mixer = pick
    for k in range(TOPK):
        same = row[:, :, k : k + 1] == lanes
        pick = jnp.where(same, 1.0, pick)
        mixer = jnp.where(same, shares[:, :, k : k + 1], mixer)
    pick, mixer = pick.astype(jnp.bfloat16), mixer.astype(jnp.bfloat16)
    everyone = gather_rows(normed).reshape(8, tokens // 8, D)
    rows = jnp.einsum("gtp,gtd->gpd", pick, everyone, preferred_element_type=jnp.float32)
    rows = rows.astype(jnp.bfloat16).reshape(8, rows_here, 32, D)
    outs = run_experts(rows, w_gate, w_up, w_down).reshape(8, rows_here * 32, D)
    part = jnp.einsum("gtp,gpd->gtd", mixer, outs, preferred_element_type=jnp.float32)
    return reduce_rows(part.astype(jnp.bfloat16).reshape(-1, tok_rows, D), stream)


def shards(
    query, new_kv, cache_kv, cached_len, residual, w_out, gain, routes, gates, w_gate, w_up, w_down
):
    tok_rows = query.shape[0]
    n_exp = lax.axis_size("exp")
    n_req = lax.axis_size("req")
    req_here = cache_kv.shape[0]
    piece_len = cache_kv.shape[1]
    kv_cols = cache_kv.shape[2] // 2
    new_len = tok_rows * n_exp // req_here
    group_index = lax.axis_index("req")
    column = lax.axis_index("exp")
    lens_group = lax.dynamic_slice_in_dim(cached_len, group_index * req_here, req_here)
    keys_local = jnp.concatenate([cache_kv.reshape(req_here * piece_len, 2 * kv_cols), new_kv], 0)
    block_rows = keys_local.shape[0]
    q_all = lax.all_gather(query, "exp", axis=0, tiled=True)
    count = q_all.shape[0]
    seen = visibility(
        jnp.arange(block_rows, dtype=jnp.int32),
        column,
        jnp.arange(count, dtype=jnp.int32),
        lens_group,
        piece_len,
        tok_rows,
        new_len,
    )
    scores = head_scores(q_all, keys_local[:, :kv_cols])
    masked = jnp.where(seen[:, None, None, :], scores, -1e30)
    peak = jnp.max(masked, axis=-1)
    expo = jnp.where(seen[:, None, None, :], jnp.exp(masked - peak[..., None]), 0.0)
    total = jnp.sum(expo, axis=-1)
    partial_value = weighted_values(expo.astype(jnp.bfloat16), keys_local[:, kv_cols:]).reshape(
        count, H * HD
    )
    peaks, totals, partials = (
        lax.all_to_all(
            peak.reshape(count, H).astype(jnp.bfloat16),
            "exp",
            split_axis=0,
            concat_axis=0,
            tiled=True,
        ).astype(jnp.float32),
        lax.all_to_all(
            total.reshape(count, H).astype(jnp.bfloat16),
            "exp",
            split_axis=0,
            concat_axis=0,
            tiled=True,
        ).astype(jnp.float32),
        lax.all_to_all(
            partial_value.astype(jnp.bfloat16), "exp", split_axis=0, concat_axis=0, tiled=True
        ).astype(partial_value.dtype),
    )
    peaks = peaks.reshape(n_exp, tok_rows, H)
    totals = totals.reshape(n_exp, tok_rows, H)
    top = jnp.max(peaks, axis=0)
    factor = jnp.exp(peaks - top[None])
    denom = jnp.sum(factor * totals, axis=0)
    numer = jnp.sum(factor[..., None] * partials.reshape(n_exp, tok_rows, H, HD), axis=0)
    attended = (numer / denom[..., None]).reshape(tok_rows, H * HD).astype(jnp.bfloat16)
    stream = (
        residual.astype(jnp.float32) + jnp.dot(attended, w_out, preferred_element_type=jnp.float32)
    ).astype(jnp.bfloat16)
    wide = stream.astype(jnp.float32)
    normed = (
        wide * lax.rsqrt(jnp.mean(wide * wide, axis=-1, keepdims=True) + 1e-06) * gain
    ).astype(jnp.bfloat16)
    rows_here = w_gate.shape[0]
    devices = n_req * n_exp
    if (n_req, n_exp, tok_rows) == (4, 8, 64):
        return routed(stream, normed, routes, gates, w_gate, w_up, w_down)
    flat = routes.reshape(-1)
    hits = (flat[:, None] == jnp.arange(EXPERTS, dtype=jnp.int32)[None, :]).astype(jnp.int32)
    slot = jnp.sum(hits * (jnp.cumsum(hits, axis=0) - 1), axis=1)
    place = flat * CAP + slot
    width = EXPERTS * CAP
    chosen = (place[:, None] == jnp.arange(width, dtype=jnp.int32)[None, :]).reshape(
        tok_rows, TOPK, width
    )
    sender = jnp.sum(chosen.astype(jnp.float32), axis=1).astype(jnp.bfloat16)
    send = jnp.einsum("tp,td->pd", sender, normed, preferred_element_type=jnp.float32).astype(
        jnp.bfloat16
    )
    send = send.reshape(EXPERTS // rows_here, rows_here * CAP, D)
    spread = jnp.concatenate([send] * HALVES, 0)
    mixer = jnp.sum(jnp.where(chosen, gates.astype(jnp.float32)[:, :, None], 0.0), axis=1).astype(
        jnp.bfloat16
    )
    arrived = lax.all_to_all(spread, ("req", "exp"), split_axis=0, concat_axis=0, tiled=True)
    pieces = arrived.reshape(devices, rows_here, CAP, D)
    gate_v = jnp.einsum("srcd,rdf->srcf", pieces, w_gate, preferred_element_type=jnp.float32)
    up_v = jnp.einsum("srcd,rdf->srcf", pieces, w_up, preferred_element_type=jnp.float32)
    hidden = (jax.nn.silu(gate_v) * up_v).astype(jnp.bfloat16)
    result = jnp.einsum("srcf,rfd->srcd", hidden, w_down, preferred_element_type=jnp.float32)
    partial_out = result.astype(jnp.bfloat16).reshape(devices, rows_here * CAP, D)
    collected = lax.all_to_all(partial_out, ("req", "exp"), split_axis=0, concat_axis=0, tiled=True)
    back = jnp.sum(collected.reshape(HALVES, width, D).astype(jnp.float32), axis=0).astype(
        jnp.bfloat16
    )
    mixed = jnp.dot(mixer, back, preferred_element_type=jnp.float32)
    return (stream.astype(jnp.float32) + mixed).astype(jnp.bfloat16)


def solution(mesh):
    return jax.shard_map(
        shards,
        mesh=mesh,
        in_specs=(
            P(("req", "exp"), None),
            P(("req", "exp"), None),
            P("req", "exp", None),
            P(),
            P(("req", "exp"), None),
            P(),
            P(),
            P(("req", "exp"), None),
            P(("req", "exp"), None),
            P(("req", "exp"), None, None),
            P(("req", "exp"), None, None),
            P(("req", "exp"), None, None),
        ),
        out_specs=P(("req", "exp"), None),
        check_vma=False,
    )
```

```python
import math

import jax
import jax.numpy as jnp
from jax import lax
from jax.experimental import pallas as pl
from jax.experimental.pallas import tpu as pltpu
from jax.sharding import PartitionSpec as P

D = 2048
H = 16
KVH = 4
HD = 128
EXPERTS = 64
TOPK = 6
HALVES = 2
CAP = 7


def visibility(key_row, key_device, query_index, lens_group, piece_len, tok_rows, new_len):
    req_here = lens_group.shape[0]
    cache_rows = req_here * piece_len
    is_cache = key_row < cache_rows
    cache_req = key_row // piece_len
    cache_pos = key_device * piece_len + key_row % piece_len
    new_token = key_device * tok_rows + key_row - cache_rows
    key_req = jnp.where(is_cache, cache_req, new_token // new_len)
    key_pos = new_token % new_len
    owners = jnp.arange(req_here, dtype=jnp.int32)
    cache_len = jnp.sum(
        jnp.where(cache_req[:, None] == owners[None, :], lens_group[None, :], 0), axis=1
    )
    query_req = query_index // new_len
    query_pos = query_index % new_len
    same = key_req[None, :] == query_req[:, None]
    seen = jnp.where(
        is_cache[None, :], (cache_pos < cache_len)[None, :], key_pos[None, :] <= query_pos[:, None]
    )
    return same & seen


def head_scores(queries, keys):
    count = queries.shape[0]
    qh = queries.reshape(count, KVH, H // KVH, HD)
    kh = keys.reshape(keys.shape[0], KVH, HD)
    return jnp.einsum("qgjd,kgd->qgjk", qh, kh, preferred_element_type=jnp.float32) * (
        1.0 / math.sqrt(HD)
    )


def weighted_values(weights, values):
    vh = values.reshape(values.shape[0], KVH, HD)
    return jnp.einsum("qgjk,kgd->qgjd", weights, vh, preferred_element_type=jnp.float32)


MESH = pl.DeviceIdType.MESH
VMEM_SPEC = pl.BlockSpec(memory_space=pltpu.VMEM)
ANY_SPEC = pl.BlockSpec(memory_space=pl.ANY)
OFFSETS = (1, 3, 2)


def place_here():
    row, col = lax.axis_index("req"), lax.axis_index("exp")
    return row // 2, col % 2, col // 2, row % 2


def peer(x, y, z, c):
    return (2 * x + c, 2 * z + y)


def block_of(x, y, z, c):
    return (2 * x + c) * 8 + 2 * z + y


def stepped(x, y, c, da, db):
    dx = jnp.where(c == 0, db, da)
    dy = jnp.where(c == 0, da, db)
    return jnp.bitwise_xor(x, dx), jnp.bitwise_xor(y, dy)


def greet(peers):
    barrier = pltpu.get_barrier_semaphore()
    for other in peers:
        pl.semaphore_signal(barrier, inc=1, device_id=other, device_id_type=MESH)
    pl.semaphore_wait(barrier, len(peers))


def partners(x, y, z, c):
    xa, ya = stepped(x, y, c, 1, 0)
    xb, yb = stepped(x, y, c, 0, 1)
    along = {k: peer(x, y, (z + k) % 4, c) for k in OFFSETS}
    return along, peer(xa, ya, z, c), peer(xb, yb, z, c), peer(x, y, z, 1 - c)


def label(da, db, k):
    return (da * 2 + db) * 4 + k


def gather_kernel(mine_ref, note_ref, out_ref, notes_ref, local_sem, send_sem, recv_sem):
    x, y, z, c = place_here()
    along, a_peer, b_peer, core_peer = partners(x, y, z, c)
    greet([*along.values(), a_peer, b_peer, core_peer])
    sent = []

    def send(src, note, block, slot, target):
        for lane, (one, dst) in enumerate(((note, notes_ref), (src, out_ref))):
            copy = pltpu.make_async_remote_copy(
                src_ref=one,
                dst_ref=dst.at[block],
                send_sem=send_sem.at[len(sent)],
                recv_sem=recv_sem.at[2 * slot + lane],
                device_id=target,
                device_id_type=MESH,
            )
            copy.start()
            sent.append(copy)

    def arrived(block, slot):
        for lane, (one, dst) in enumerate(((note_ref, notes_ref), (mine_ref, out_ref))):
            pltpu.make_async_remote_copy(
                src_ref=one,
                dst_ref=dst.at[block],
                send_sem=send_sem.at[0],
                recv_sem=recv_sem.at[2 * slot + lane],
                device_id=core_peer,
                device_id_type=MESH,
            ).wait_recv()

    def block(da, db, k):
        xs, ys = stepped(x, y, c, da, db)
        return block_of(xs, ys, (z + k) % 4, c)

    own = block_of(x, y, z, c)
    send(mine_ref, note_ref, own, label(0, 1, 0), b_peer)
    send(mine_ref, note_ref, own, label(1, 0, 0), a_peer)
    for k in OFFSETS:
        send(mine_ref, note_ref, own, label(0, 0, (4 - k) % 4), along[k])
    send(mine_ref, note_ref, own, 16 + label(0, 0, 0), core_peer)
    keep = pltpu.make_async_copy(mine_ref, out_ref.at[own], local_sem.at[0])
    keep.start()
    jot = pltpu.make_async_copy(note_ref, notes_ref.at[own], local_sem.at[1])
    jot.start()

    def relay(da, db, k):
        b = block(da, db, k)
        arrived(b, label(da, db, k))
        if db == 0:
            send(out_ref.at[b], notes_ref.at[b], b, label(da, 1, k), b_peer)
            if da == 0:
                send(out_ref.at[b], notes_ref.at[b], b, label(1, 0, k), a_peer)
        send(out_ref.at[b], notes_ref.at[b], b, 16 + label(da, db, k), core_peer)

    relay(1, 0, 0)
    for k in OFFSETS:
        relay(0, 0, k)
    relay(0, 1, 0)
    for k in OFFSETS:
        relay(1, 0, k)
    relay(1, 1, 0)
    for k in OFFSETS:
        relay(0, 1, k)
    for k in OFFSETS:
        relay(1, 1, k)
    for da in range(2):
        for db in range(2):
            for k in range(4):
                xs, ys = stepped(x, y, 1 - c, da, db)
                arrived(block_of(xs, ys, (z + k) % 4, 1 - c), 16 + label(da, db, k))
    keep.wait()
    jot.wait()
    for copy in sent:
        copy.wait_send()


def gather_rows(mine, note):
    whole = lambda one: jax.ShapeDtypeStruct((32, *one.shape), one.dtype)
    return pl.pallas_call(
        gather_kernel,
        out_shape=(whole(mine), whole(note)),
        in_specs=[VMEM_SPEC, VMEM_SPEC],
        out_specs=(ANY_SPEC, ANY_SPEC),
        scratch_shapes=[
            pltpu.SemaphoreType.DMA((2,)),
            pltpu.SemaphoreType.DMA((62,)),
            pltpu.SemaphoreType.DMA((64,)),
        ],
        compiler_params=pltpu.CompilerParams(collective_id=1, has_side_effects=True),
        name="gather_rows",
    )(mine, note)


def reduce_kernel(
    part_ref, stream_ref, out_ref, in_c, in_b, in_a, in_z, sum_c, sum_b, sum_a, send_sem, recv_sem
):
    x, y, z, c = place_here()
    along, a_peer, b_peer, core_peer = partners(x, y, z, c)
    greet([*along.values(), a_peer, b_peer, core_peer])
    sent = []
    f32 = jnp.float32

    def send(src, dst, slot, target):
        copy = pltpu.make_async_remote_copy(
            src_ref=src,
            dst_ref=dst,
            send_sem=send_sem.at[len(sent)],
            recv_sem=recv_sem.at[slot],
            device_id=target,
            device_id_type=MESH,
        )
        copy.start()
        sent.append(copy)

    def arrived(dst, slot):
        pltpu.make_async_remote_copy(
            src_ref=dst,
            dst_ref=dst,
            send_sem=send_sem.at[0],
            recv_sem=recv_sem.at[slot],
            device_id=core_peer,
            device_id_type=MESH,
        ).wait_recv()

    def add(dst, one, two):
        rows = dst.shape[0]

        @pl.loop(0, rows // 16)
        def _(i):
            part = pl.ds(pl.multiple_of(i * 16, 16), 16)
            dst[part, :] = (one[part, :].astype(f32) + two[part, :].astype(f32)).astype(dst.dtype)

    ks = (*OFFSETS, 0)
    order = [(da, db, k) for db in (1, 0) for da in (1, 0) for k in ks]
    for da, db, k in order:
        xs, ys = stepped(x, y, 1 - c, da, db)
        i = label(da, db, k)
        send(part_ref.at[block_of(xs, ys, (z + k) % 4, 1 - c)], in_c.at[i], i, core_peer)
    for da, db, k in order:
        i = label(da, db, k)
        xs, ys = stepped(x, y, c, da, db)
        arrived(in_c.at[i], i)
        add(sum_c.at[i], part_ref.at[block_of(xs, ys, (z + k) % 4, c)], in_c.at[i])
        if db == 1:
            send(sum_c.at[i], in_b.at[da * 4 + k], 16 + da * 4 + k, b_peer)
    for da in (1, 0):
        for k in ks:
            j = da * 4 + k
            arrived(in_b.at[j], 16 + j)
            add(sum_b.at[j], sum_c.at[label(da, 0, k)], in_b.at[j])
            if da == 1:
                send(sum_b.at[j], in_a.at[k], 24 + k, a_peer)
    for k in ks:
        arrived(in_a.at[k], 24 + k)
        add(sum_a.at[k], sum_b.at[k], in_a.at[k])
        if k:
            send(sum_a.at[k], in_z.at[4 - k], 28 + (4 - k), along[k])
    for k in OFFSETS:
        arrived(in_z.at[k], 28 + k)
    rows = out_ref.shape[0]

    @pl.loop(0, rows // 16)
    def _(i):
        part = pl.ds(pl.multiple_of(i * 16, 16), 16)
        whole = sum_a[0, part, :].astype(f32)
        for k in OFFSETS:
            whole += in_z[k, part, :].astype(f32)
        out_ref[part, :] = (stream_ref[part, :].astype(f32) + whole).astype(out_ref.dtype)

    for copy in sent:
        copy.wait_send()


def reduce_rows(part, stream):
    rows, width = stream.shape
    space = lambda n: pltpu.VMEM((n, rows, width), jnp.bfloat16)
    return pl.pallas_call(
        reduce_kernel,
        out_shape=jax.ShapeDtypeStruct(stream.shape, stream.dtype),
        in_specs=[VMEM_SPEC, VMEM_SPEC],
        out_specs=VMEM_SPEC,
        scratch_shapes=[
            space(16),
            space(8),
            space(4),
            space(4),
            space(16),
            space(8),
            space(4),
            pltpu.SemaphoreType.DMA((31,)),
            pltpu.SemaphoreType.DMA((32,)),
        ],
        compiler_params=pltpu.CompilerParams(
            collective_id=2, has_side_effects=True, vmem_limit_bytes=48 * 2**20
        ),
        name="reduce_rows",
    )(part, stream)


def expert_kernel(rows_ref, gate_ref, up_ref, down_ref, out_ref):
    groups, _, count, width = rows_ref.shape
    rows = rows_ref[...].reshape(groups * count, width)
    across = (((1,), (1,)), ((), ()))
    gate = lax.dot_general(rows, gate_ref[0], across, preferred_element_type=jnp.float32)
    up = lax.dot_general(rows, up_ref[0], across, preferred_element_type=jnp.float32)
    hidden = (gate / (1.0 + jnp.exp(-gate)) * up).astype(jnp.bfloat16)
    part = jnp.dot(hidden, down_ref[0], preferred_element_type=jnp.float32)
    out_ref[...] = part.astype(jnp.bfloat16).reshape(groups, 1, count, width)


def run_experts(rows, w_gate, w_up, w_down):
    groups, here, count, width = rows.shape
    ff = w_gate.shape[2]
    lot = pl.BlockSpec((groups, 1, count, width), lambda r: (0, r, 0, 0))
    return pl.pallas_call(
        expert_kernel,
        out_shape=jax.ShapeDtypeStruct(rows.shape, rows.dtype),
        grid=(here,),
        in_specs=[
            lot,
            pl.BlockSpec((1, ff, width), lambda r: (r, 0, 0)),
            pl.BlockSpec((1, ff, width), lambda r: (r, 0, 0)),
            pl.BlockSpec((1, ff, width), lambda r: (r, 0, 0)),
        ],
        out_specs=lot,
        compiler_params=pltpu.CompilerParams(vmem_limit_bytes=48 * 2**20),
        name="run_experts",
    )(rows, w_gate.swapaxes(1, 2), w_up.swapaxes(1, 2), w_down)


def routed(stream, normed, routes, gates, w_gate, w_up, w_down):
    tok_rows = stream.shape[0]
    rows_here = w_gate.shape[0]
    me = lax.axis_index("req") * lax.axis_size("exp") + lax.axis_index("exp")
    flat = routes.reshape(-1)
    hits = (flat[:, None] == jnp.arange(EXPERTS, dtype=jnp.int32)[None, :]).astype(jnp.int32)
    slot = jnp.sum(hits * (jnp.cumsum(hits, axis=0) - 1), axis=1)
    note = jnp.concatenate(
        [routes.astype(gates.dtype), slot.reshape(tok_rows, TOPK).astype(gates.dtype), gates], 1
    )
    note = jnp.pad(note, ((0, 0), (0, 128 - 3 * TOPK)))
    everyone, notes = gather_rows(normed, note)
    tokens = everyone.shape[0] * tok_rows
    everyone = everyone.reshape(8, tokens // 8, D)
    notes = notes.reshape(tokens, 128).astype(jnp.float32)
    places = (notes[:, :TOPK] * CAP + notes[:, TOPK : 2 * TOPK]).astype(jnp.int32)
    shares = notes[:, 2 * TOPK : 3 * TOPK]
    first = me * rows_here % EXPERTS * CAP
    rel = places - first
    lot = jnp.arange(tokens, dtype=jnp.int32)[:, None] // tok_rows % 4
    row = rel // CAP * 32 + lot * CAP + rel % CAP
    row = jnp.where((rel >= 0) & (rel < rows_here * CAP), row, -1).reshape(8, tokens // 8, TOPK)
    shares = shares.reshape(8, tokens // 8, TOPK)
    lanes = jnp.arange(rows_here * 32, dtype=jnp.int32)
    pick = jnp.zeros((8, tokens // 8, rows_here * 32), jnp.float32)
    mixer = pick
    for k in range(TOPK):
        same = row[:, :, k : k + 1] == lanes
        pick = jnp.where(same, 1.0, pick)
        mixer = jnp.where(same, shares[:, :, k : k + 1], mixer)
    pick, mixer = pick.astype(jnp.bfloat16), mixer.astype(jnp.bfloat16)
    rows = jnp.einsum("gtp,gtd->gpd", pick, everyone, preferred_element_type=jnp.float32)
    rows = rows.astype(jnp.bfloat16).reshape(8, rows_here, 32, D)
    outs = run_experts(rows, w_gate, w_up, w_down).reshape(8, rows_here * 32, D)
    part = jnp.einsum("gtp,gpd->gtd", mixer, outs, preferred_element_type=jnp.float32)
    return reduce_rows(part.astype(jnp.bfloat16).reshape(-1, tok_rows, D), stream)


def shards(
    query, new_kv, cache_kv, cached_len, residual, w_out, gain, routes, gates, w_gate, w_up, w_down
):
    tok_rows = query.shape[0]
    n_exp = lax.axis_size("exp")
    n_req = lax.axis_size("req")
    req_here = cache_kv.shape[0]
    piece_len = cache_kv.shape[1]
    kv_cols = cache_kv.shape[2] // 2
    new_len = tok_rows * n_exp // req_here
    group_index = lax.axis_index("req")
    column = lax.axis_index("exp")
    lens_group = lax.dynamic_slice_in_dim(cached_len, group_index * req_here, req_here)
    keys_local = jnp.concatenate([cache_kv.reshape(req_here * piece_len, 2 * kv_cols), new_kv], 0)
    block_rows = keys_local.shape[0]
    q_all = lax.all_gather(query, "exp", axis=0, tiled=True)
    count = q_all.shape[0]
    seen = visibility(
        jnp.arange(block_rows, dtype=jnp.int32),
        column,
        jnp.arange(count, dtype=jnp.int32),
        lens_group,
        piece_len,
        tok_rows,
        new_len,
    )
    scores = head_scores(q_all, keys_local[:, :kv_cols])
    masked = jnp.where(seen[:, None, None, :], scores, -1e30)
    peak = jnp.max(masked, axis=-1)
    expo = jnp.where(seen[:, None, None, :], jnp.exp(masked - peak[..., None]), 0.0)
    total = jnp.sum(expo, axis=-1)
    partial_value = weighted_values(expo.astype(jnp.bfloat16), keys_local[:, kv_cols:]).reshape(
        count, H * HD
    )
    peaks, totals, partials = (
        lax.all_to_all(
            peak.reshape(count, H).astype(jnp.bfloat16),
            "exp",
            split_axis=0,
            concat_axis=0,
            tiled=True,
        ).astype(jnp.float32),
        lax.all_to_all(
            total.reshape(count, H).astype(jnp.bfloat16),
            "exp",
            split_axis=0,
            concat_axis=0,
            tiled=True,
        ).astype(jnp.float32),
        lax.all_to_all(
            partial_value.astype(jnp.bfloat16), "exp", split_axis=0, concat_axis=0, tiled=True
        ).astype(partial_value.dtype),
    )
    peaks = peaks.reshape(n_exp, tok_rows, H)
    totals = totals.reshape(n_exp, tok_rows, H)
    top = jnp.max(peaks, axis=0)
    factor = jnp.exp(peaks - top[None])
    denom = jnp.sum(factor * totals, axis=0)
    numer = jnp.sum(factor[..., None] * partials.reshape(n_exp, tok_rows, H, HD), axis=0)
    attended = (numer / denom[..., None]).reshape(tok_rows, H * HD).astype(jnp.bfloat16)
    stream = (
        residual.astype(jnp.float32) + jnp.dot(attended, w_out, preferred_element_type=jnp.float32)
    ).astype(jnp.bfloat16)
    wide = stream.astype(jnp.float32)
    normed = (
        wide * lax.rsqrt(jnp.mean(wide * wide, axis=-1, keepdims=True) + 1e-06) * gain
    ).astype(jnp.bfloat16)
    rows_here = w_gate.shape[0]
    devices = n_req * n_exp
    if (n_req, n_exp, tok_rows) == (4, 8, 64):
        return routed(stream, normed, routes, gates, w_gate, w_up, w_down)
    flat = routes.reshape(-1)
    hits = (flat[:, None] == jnp.arange(EXPERTS, dtype=jnp.int32)[None, :]).astype(jnp.int32)
    slot = jnp.sum(hits * (jnp.cumsum(hits, axis=0) - 1), axis=1)
    place = flat * CAP + slot
    width = EXPERTS * CAP
    chosen = (place[:, None] == jnp.arange(width, dtype=jnp.int32)[None, :]).reshape(
        tok_rows, TOPK, width
    )
    sender = jnp.sum(chosen.astype(jnp.float32), axis=1).astype(jnp.bfloat16)
    send = jnp.einsum("tp,td->pd", sender, normed, preferred_element_type=jnp.float32).astype(
        jnp.bfloat16
    )
    send = send.reshape(EXPERTS // rows_here, rows_here * CAP, D)
    spread = jnp.concatenate([send] * HALVES, 0)
    mixer = jnp.sum(jnp.where(chosen, gates.astype(jnp.float32)[:, :, None], 0.0), axis=1).astype(
        jnp.bfloat16
    )
    arrived = lax.all_to_all(spread, ("req", "exp"), split_axis=0, concat_axis=0, tiled=True)
    pieces = arrived.reshape(devices, rows_here, CAP, D)
    gate_v = jnp.einsum("srcd,rdf->srcf", pieces, w_gate, preferred_element_type=jnp.float32)
    up_v = jnp.einsum("srcd,rdf->srcf", pieces, w_up, preferred_element_type=jnp.float32)
    hidden = (jax.nn.silu(gate_v) * up_v).astype(jnp.bfloat16)
    result = jnp.einsum("srcf,rfd->srcd", hidden, w_down, preferred_element_type=jnp.float32)
    partial_out = result.astype(jnp.bfloat16).reshape(devices, rows_here * CAP, D)
    collected = lax.all_to_all(partial_out, ("req", "exp"), split_axis=0, concat_axis=0, tiled=True)
    back = jnp.sum(collected.reshape(HALVES, width, D).astype(jnp.float32), axis=0).astype(
        jnp.bfloat16
    )
    mixed = jnp.dot(mixer, back, preferred_element_type=jnp.float32)
    return (stream.astype(jnp.float32) + mixed).astype(jnp.bfloat16)


def solution(mesh):
    return jax.shard_map(
        shards,
        mesh=mesh,
        in_specs=(
            P(("req", "exp"), None),
            P(("req", "exp"), None),
            P("req", "exp", None),
            P(),
            P(("req", "exp"), None),
            P(),
            P(),
            P(("req", "exp"), None),
            P(("req", "exp"), None),
            P(("req", "exp"), None, None),
            P(("req", "exp"), None, None),
            P(("req", "exp"), None, None),
        ),
        out_specs=P(("req", "exp"), None),
        check_vma=False,
    )
```

```python
import math

import jax
import jax.numpy as jnp
from jax import lax
from jax.experimental import pallas as pl
from jax.experimental.pallas import tpu as pltpu
from jax.sharding import PartitionSpec as P

D = 2048
H = 16
KVH = 4
HD = 128
EXPERTS = 64
TOPK = 6
HALVES = 2
CAP = 7


def visibility(key_row, key_device, query_index, lens_group, piece_len, tok_rows, new_len):
    req_here = lens_group.shape[0]
    cache_rows = req_here * piece_len
    is_cache = key_row < cache_rows
    cache_req = key_row // piece_len
    cache_pos = key_device * piece_len + key_row % piece_len
    new_token = key_device * tok_rows + key_row - cache_rows
    key_req = jnp.where(is_cache, cache_req, new_token // new_len)
    key_pos = new_token % new_len
    owners = jnp.arange(req_here, dtype=jnp.int32)
    cache_len = jnp.sum(
        jnp.where(cache_req[:, None] == owners[None, :], lens_group[None, :], 0), axis=1
    )
    query_req = query_index // new_len
    query_pos = query_index % new_len
    same = key_req[None, :] == query_req[:, None]
    seen = jnp.where(
        is_cache[None, :], (cache_pos < cache_len)[None, :], key_pos[None, :] <= query_pos[:, None]
    )
    return same & seen


def head_scores(queries, keys):
    count = queries.shape[0]
    qh = queries.reshape(count, KVH, H // KVH, HD)
    kh = keys.reshape(keys.shape[0], KVH, HD)
    return jnp.einsum("qgjd,kgd->qgjk", qh, kh, preferred_element_type=jnp.float32) * (
        1.0 / math.sqrt(HD)
    )


def weighted_values(weights, values):
    vh = values.reshape(values.shape[0], KVH, HD)
    return jnp.einsum("qgjk,kgd->qgjd", weights, vh, preferred_element_type=jnp.float32)


MESH = pl.DeviceIdType.MESH
VMEM_SPEC = pl.BlockSpec(memory_space=pltpu.VMEM)
ANY_SPEC = pl.BlockSpec(memory_space=pl.ANY)
OFFSETS = (1, 3, 2)


def place_here():
    row, col = lax.axis_index("req"), lax.axis_index("exp")
    return row // 2, col % 2, col // 2, row % 2


def peer(x, y, z, c):
    return (2 * x + c, 2 * z + y)


def block_of(x, y, z, c):
    return (2 * x + c) * 8 + 2 * z + y


def stepped(x, y, c, da, db):
    dx = jnp.where(c == 0, db, da)
    dy = jnp.where(c == 0, da, db)
    return jnp.bitwise_xor(x, dx), jnp.bitwise_xor(y, dy)


def greet(peers):
    barrier = pltpu.get_barrier_semaphore()
    for other in peers:
        pl.semaphore_signal(barrier, inc=1, device_id=other, device_id_type=MESH)
    pl.semaphore_wait(barrier, len(peers))


def partners(x, y, z, c):
    xa, ya = stepped(x, y, c, 1, 0)
    xb, yb = stepped(x, y, c, 0, 1)
    along = {k: peer(x, y, (z + k) % 4, c) for k in OFFSETS}
    return along, peer(xa, ya, z, c), peer(xb, yb, z, c), peer(x, y, z, 1 - c)


def label(da, db, k):
    return (da * 2 + db) * 4 + k


def gather_kernel(mine_ref, note_ref, out_ref, notes_ref, local_sem, send_sem, recv_sem):
    x, y, z, c = place_here()
    along, a_peer, b_peer, core_peer = partners(x, y, z, c)
    greet([*along.values(), a_peer, b_peer, core_peer])
    sent = []

    def send(src, note, block, slot, target):
        for lane, (one, dst) in enumerate(((note, notes_ref), (src, out_ref))):
            copy = pltpu.make_async_remote_copy(
                src_ref=one,
                dst_ref=dst.at[block],
                send_sem=send_sem.at[len(sent)],
                recv_sem=recv_sem.at[2 * slot + lane],
                device_id=target,
                device_id_type=MESH,
            )
            copy.start()
            sent.append(copy)

    def arrived(block, slot):
        for lane, (one, dst) in enumerate(((note_ref, notes_ref), (mine_ref, out_ref))):
            pltpu.make_async_remote_copy(
                src_ref=one,
                dst_ref=dst.at[block],
                send_sem=send_sem.at[0],
                recv_sem=recv_sem.at[2 * slot + lane],
                device_id=core_peer,
                device_id_type=MESH,
            ).wait_recv()

    def block(da, db, k):
        xs, ys = stepped(x, y, c, da, db)
        return block_of(xs, ys, (z + k) % 4, c)

    own = block_of(x, y, z, c)
    send(mine_ref, note_ref, own, label(0, 1, 0), b_peer)
    send(mine_ref, note_ref, own, label(1, 0, 0), a_peer)
    for k in OFFSETS:
        send(mine_ref, note_ref, own, label(0, 0, (4 - k) % 4), along[k])
    send(mine_ref, note_ref, own, 16 + label(0, 0, 0), core_peer)
    keep = pltpu.make_async_copy(mine_ref, out_ref.at[own], local_sem.at[0])
    keep.start()
    jot = pltpu.make_async_copy(note_ref, notes_ref.at[own], local_sem.at[1])
    jot.start()

    def relay(da, db, k):
        b = block(da, db, k)
        arrived(b, label(da, db, k))
        if db == 0:
            send(out_ref.at[b], notes_ref.at[b], b, label(da, 1, k), b_peer)
            if da == 0:
                send(out_ref.at[b], notes_ref.at[b], b, label(1, 0, k), a_peer)
        send(out_ref.at[b], notes_ref.at[b], b, 16 + label(da, db, k), core_peer)

    relay(1, 0, 0)
    for k in OFFSETS:
        relay(0, 0, k)
    relay(0, 1, 0)
    for k in OFFSETS:
        relay(1, 0, k)
    relay(1, 1, 0)
    for k in OFFSETS:
        relay(0, 1, k)
    for k in OFFSETS:
        relay(1, 1, k)
    for da in range(2):
        for db in range(2):
            for k in range(4):
                xs, ys = stepped(x, y, 1 - c, da, db)
                arrived(block_of(xs, ys, (z + k) % 4, 1 - c), 16 + label(da, db, k))
    keep.wait()
    jot.wait()
    for copy in sent:
        copy.wait_send()


def gather_rows(mine, note):
    whole = lambda one: jax.ShapeDtypeStruct((32, *one.shape), one.dtype)
    return pl.pallas_call(
        gather_kernel,
        out_shape=(whole(mine), whole(note)),
        in_specs=[VMEM_SPEC, VMEM_SPEC],
        out_specs=(ANY_SPEC, ANY_SPEC),
        scratch_shapes=[
            pltpu.SemaphoreType.DMA((2,)),
            pltpu.SemaphoreType.DMA((62,)),
            pltpu.SemaphoreType.DMA((64,)),
        ],
        compiler_params=pltpu.CompilerParams(collective_id=1, has_side_effects=True),
        name="gather_rows",
    )(mine, note)


def reduce_kernel(
    part_ref, stream_ref, out_ref, in_c, in_b, in_a, in_z, sum_c, sum_b, sum_a, send_sem, recv_sem
):
    x, y, z, c = place_here()
    along, a_peer, b_peer, core_peer = partners(x, y, z, c)
    greet([*along.values(), a_peer, b_peer, core_peer])
    sent = []
    f32 = jnp.float32

    def send(src, dst, slot, target):
        copy = pltpu.make_async_remote_copy(
            src_ref=src,
            dst_ref=dst,
            send_sem=send_sem.at[len(sent)],
            recv_sem=recv_sem.at[slot],
            device_id=target,
            device_id_type=MESH,
        )
        copy.start()
        sent.append(copy)

    def arrived(dst, slot):
        pltpu.make_async_remote_copy(
            src_ref=dst,
            dst_ref=dst,
            send_sem=send_sem.at[0],
            recv_sem=recv_sem.at[slot],
            device_id=core_peer,
            device_id_type=MESH,
        ).wait_recv()

    def add(dst, one, two):
        rows = dst.shape[0]

        @pl.loop(0, rows // 16)
        def _(i):
            part = pl.ds(pl.multiple_of(i * 16, 16), 16)
            dst[part, :] = (one[part, :].astype(f32) + two[part, :].astype(f32)).astype(dst.dtype)

    ks = (*OFFSETS, 0)
    order = [(da, db, k) for db in (1, 0) for da in (1, 0) for k in ks]
    for da, db, k in order:
        xs, ys = stepped(x, y, 1 - c, da, db)
        i = label(da, db, k)
        send(part_ref.at[block_of(xs, ys, (z + k) % 4, 1 - c)], in_c.at[i], i, core_peer)
    for da, db, k in order:
        i = label(da, db, k)
        xs, ys = stepped(x, y, c, da, db)
        arrived(in_c.at[i], i)
        add(sum_c.at[i], part_ref.at[block_of(xs, ys, (z + k) % 4, c)], in_c.at[i])
        if db == 1:
            send(sum_c.at[i], in_b.at[da * 4 + k], 16 + da * 4 + k, b_peer)
    for da in (1, 0):
        for k in ks:
            j = da * 4 + k
            arrived(in_b.at[j], 16 + j)
            add(sum_b.at[j], sum_c.at[label(da, 0, k)], in_b.at[j])
            if da == 1:
                send(sum_b.at[j], in_a.at[k], 24 + k, a_peer)
    for k in ks:
        arrived(in_a.at[k], 24 + k)
        add(sum_a.at[k], sum_b.at[k], in_a.at[k])
        if k:
            send(sum_a.at[k], in_z.at[4 - k], 28 + (4 - k), along[k])
    for k in OFFSETS:
        arrived(in_z.at[k], 28 + k)
    rows = out_ref.shape[0]

    @pl.loop(0, rows // 16)
    def _(i):
        part = pl.ds(pl.multiple_of(i * 16, 16), 16)
        whole = sum_a[0, part, :].astype(f32)
        for k in OFFSETS:
            whole += in_z[k, part, :].astype(f32)
        out_ref[part, :] = (stream_ref[part, :].astype(f32) + whole).astype(out_ref.dtype)

    for copy in sent:
        copy.wait_send()


def reduce_rows(part, stream):
    rows, width = stream.shape
    space = lambda n: pltpu.VMEM((n, rows, width), jnp.bfloat16)
    return pl.pallas_call(
        reduce_kernel,
        out_shape=jax.ShapeDtypeStruct(stream.shape, stream.dtype),
        in_specs=[VMEM_SPEC, VMEM_SPEC],
        out_specs=VMEM_SPEC,
        scratch_shapes=[
            space(16),
            space(8),
            space(4),
            space(4),
            space(16),
            space(8),
            space(4),
            pltpu.SemaphoreType.DMA((31,)),
            pltpu.SemaphoreType.DMA((32,)),
        ],
        compiler_params=pltpu.CompilerParams(
            collective_id=2, has_side_effects=True, vmem_limit_bytes=48 * 2**20
        ),
        name="reduce_rows",
    )(part, stream)


def expert_kernel(rows_ref, gate_ref, up_ref, down_ref, out_ref):
    groups, _, count, width = rows_ref.shape
    rows = rows_ref[...].reshape(groups * count, width)
    across = (((1,), (1,)), ((), ()))
    gate = lax.dot_general(rows, gate_ref[0], across, preferred_element_type=jnp.float32)
    up = lax.dot_general(rows, up_ref[0], across, preferred_element_type=jnp.float32)
    hidden = (gate / (1.0 + jnp.exp(-gate)) * up).astype(jnp.bfloat16)
    part = jnp.dot(hidden, down_ref[0], preferred_element_type=jnp.float32)
    out_ref[...] = part.astype(jnp.bfloat16).reshape(groups, 1, count, width)


def run_experts(rows, w_gate, w_up, w_down):
    groups, here, count, width = rows.shape
    ff = w_gate.shape[2]
    lot = pl.BlockSpec((groups, 1, count, width), lambda r: (0, r, 0, 0))
    return pl.pallas_call(
        expert_kernel,
        out_shape=jax.ShapeDtypeStruct(rows.shape, rows.dtype),
        grid=(here,),
        in_specs=[
            lot,
            pl.BlockSpec((1, ff, width), lambda r: (r, 0, 0)),
            pl.BlockSpec((1, ff, width), lambda r: (r, 0, 0)),
            pl.BlockSpec((1, ff, width), lambda r: (r, 0, 0)),
        ],
        out_specs=lot,
        compiler_params=pltpu.CompilerParams(vmem_limit_bytes=48 * 2**20),
        name="run_experts",
    )(rows, w_gate.swapaxes(1, 2), w_up.swapaxes(1, 2), w_down)


def routed(stream, normed, routes, gates, w_gate, w_up, w_down):
    tok_rows = stream.shape[0]
    rows_here = w_gate.shape[0]
    me = lax.axis_index("req") * lax.axis_size("exp") + lax.axis_index("exp")
    flat = routes.reshape(-1)
    hits = (flat[:, None] == jnp.arange(EXPERTS, dtype=jnp.int32)[None, :]).astype(jnp.int32)
    slot = jnp.sum(hits * (jnp.cumsum(hits, axis=0) - 1), axis=1)
    note = jnp.concatenate(
        [routes.astype(gates.dtype), slot.reshape(tok_rows, TOPK).astype(gates.dtype), gates], 1
    )
    note = jnp.pad(note, ((0, 0), (0, 128 - 3 * TOPK)))
    everyone, notes = gather_rows(normed, note)
    tokens = everyone.shape[0] * tok_rows
    everyone = everyone.reshape(8, tokens // 8, D)
    notes = notes.reshape(tokens, 128).astype(jnp.float32)
    places = (notes[:, :TOPK] * CAP + notes[:, TOPK : 2 * TOPK]).astype(jnp.int32)
    shares = notes[:, 2 * TOPK : 3 * TOPK]
    first = me * rows_here % EXPERTS * CAP
    rel = places - first
    lot = jnp.arange(tokens, dtype=jnp.int32)[:, None] // tok_rows % 4
    row = rel // CAP * 32 + lot * CAP + rel % CAP
    row = jnp.where((rel >= 0) & (rel < rows_here * CAP), row, -1).reshape(8, tokens // 8, TOPK)
    shares = shares.reshape(8, tokens // 8, TOPK)
    lanes = jnp.arange(rows_here * 32, dtype=jnp.int32)
    pick = jnp.zeros((8, tokens // 8, rows_here * 32), jnp.float32)
    mixer = pick
    for k in range(TOPK):
        same = row[:, :, k : k + 1] == lanes
        pick = jnp.where(same, 1.0, pick)
        mixer = jnp.where(same, shares[:, :, k : k + 1], mixer)
    pick, mixer = pick.astype(jnp.bfloat16), mixer.astype(jnp.bfloat16)
    rows = jnp.einsum("gtp,gtd->gpd", pick, everyone, preferred_element_type=jnp.float32)
    rows = rows.astype(jnp.bfloat16).reshape(8, rows_here, 32, D)
    outs = run_experts(rows, w_gate, w_up, w_down).reshape(8, rows_here * 32, D)
    part = jnp.einsum("gtp,gpd->gtd", mixer, outs, preferred_element_type=jnp.float32)
    return reduce_rows(part.astype(jnp.bfloat16).reshape(-1, tok_rows, D), stream)


def attend_kernel(
    q_ref, new_ref, cache_ref, lim_ref, out_ref,
    q_all, keys, values, out_n, out_s, in_n, in_s, local_sem, send_sem, recv_sem,
):
    row, me = lax.axis_index("req"), lax.axis_index("exp")
    f32 = jnp.float32
    bits = jnp.bitwise_xor
    greet([(row, bits(me, off)) for off in range(1, 8)])
    tok, fresh = q_ref.shape[0], cache_ref.shape[1]
    span = q_ref.shape[1] // KVH
    kv_cols = KVH * HD

    def pieces(head):
        at = lambda first: pl.ds(pl.multiple_of(first + head * HD, HD), HD)
        lot = me % 4
        old, new = pl.ds(0, fresh), pl.ds(fresh, tok)
        return (
            (cache_ref.at[0, :, at(0)], keys.at[lot, old, :]),
            (new_ref.at[:, at(0)], keys.at[lot, new, :]),
            (cache_ref.at[0, :, at(kv_cols)], values.at[lot, old, :]),
            (new_ref.at[:, at(kv_cols)], values.at[lot, new, :]),
        )

    def remote(src, dst, out_slot, in_slot, target):
        return pltpu.make_async_remote_copy(
            src_ref=src,
            dst_ref=dst,
            send_sem=send_sem.at[out_slot],
            recv_sem=recv_sem.at[in_slot],
            device_id=(row, target),
            device_id_type=MESH,
        )

    def q_piece(head):
        return q_ref.at[:, pl.ds(pl.multiple_of(head * span, span), span)]

    sent, local = [], []
    for off in (3, 2, 1):
        other = bits(me, off)
        for i, (src, dst) in enumerate(pieces(other % 4)):
            n = 8 + off * 4 + i
            sent.append(remote(src, dst, n, n, other))
            sent[-1].start()
    for off in (7, 6, 5, 4, 3, 2, 1):
        other = bits(me, off)
        sent.append(remote(q_piece(other % 4), q_all.at[me], off, off, other))
        sent[-1].start()
    for i, (src, dst) in enumerate((*pieces(me % 4), (q_piece(me % 4), q_all.at[me]))):
        local.append(pltpu.make_async_copy(src, dst, local_sem.at[i]))
        local[-1].start()
    for copy in local:
        copy.wait()
    for off in (1, 2, 3):
        lot = bits(me, off) % 4
        old, new = pl.ds(0, fresh), pl.ds(fresh, tok)
        lands = (keys.at[lot, old, :], keys.at[lot, new, :], values.at[lot, old, :], values.at[lot, new, :])
        for i, dst in enumerate(lands):
            n = 8 + off * 4 + i
            remote(dst, dst, n, n, bits(me, off)).wait_recv()

    def attend(owner):
        q = q_all[owner]
        group = H // KVH
        stacked = jnp.concatenate([q[:, h * HD : (h + 1) * HD] for h in range(group)], 0)
        k = keys[...].reshape(-1, HD)
        v = values[...].reshape(-1, HD)
        across = (((1,), (1,)), ((), ()))
        scores = lax.dot_general(stacked, k, across, preferred_element_type=f32)
        scores = scores * (1.0 / math.sqrt(HD))
        here = owner * tok + lax.broadcasted_iota(jnp.int32, (group * tok, 1), 0) % tok
        seen = lim_ref[...] <= here
        masked = jnp.where(seen, scores, -1e30)
        peak = jnp.max(masked, axis=1, keepdims=True)
        expo = jnp.where(seen, jnp.exp(masked - peak), 0.0)
        total = jnp.sum(expo, axis=1, keepdims=True)
        numer = jnp.dot(expo.astype(jnp.bfloat16), v, preferred_element_type=f32)
        lane = lax.broadcasted_iota(jnp.int32, (tok, 128), 1)
        stats = jnp.zeros((tok, 128), f32)
        parts = []
        for h in range(group):
            rows = slice(h * tok, (h + 1) * tok)
            stats = jnp.where(lane == h, peak[rows], stats)
            stats = jnp.where(lane == group + h, total[rows], stats)
            parts.append(numer[rows])
        return jnp.concatenate(parts, 1).astype(jnp.bfloat16), stats

    @pl.loop(0, 7)
    def _(step):
        off = 7 - step
        owner = bits(me, off)
        remote(q_all.at[owner], q_all.at[owner], off, off, owner).wait_recv()
        numer, stats = attend(owner)
        out_n[step] = numer
        out_s[step] = stats
        remote(out_n.at[step], in_n.at[me], 24 + off, 24 + off, owner).start()
        remote(out_s.at[step], in_s.at[me], 32 + off, 32 + off, owner).start()

    numer, stats = attend(me)
    in_n[me] = numer
    in_s[me] = stats
    for off in range(1, 8):
        other = bits(me, off)
        remote(in_n.at[other], in_n.at[other], 24 + off, 24 + off, other).wait_recv()
        remote(in_s.at[other], in_s.at[other], 32 + off, 32 + off, other).wait_recv()
    group = H // KVH
    for head in range(KVH):
        one, two = in_s[head], in_s[KVH + head]
        for h in range(group):
            p1, p2 = one[:, h : h + 1], two[:, h : h + 1]
            top = jnp.maximum(p1, p2)
            f1, f2 = jnp.exp(p1 - top), jnp.exp(p2 - top)
            denom = f1 * one[:, group + h : group + h + 1] + f2 * two[:, group + h : group + h + 1]
            cols = slice(h * HD, (h + 1) * HD)
            numer = f1 * in_n[head, :, cols].astype(f32) + f2 * in_n[KVH + head, :, cols].astype(f32)
            at = (head * group + h) * HD
            out_ref[:, at : at + HD] = (numer / denom).astype(out_ref.dtype)
    for copy in sent:
        copy.wait_send()
    for off in range(1, 8):
        remote(out_n.at[7 - off], in_n.at[me], 24 + off, 24 + off, bits(me, off)).wait_send()
        remote(out_s.at[7 - off], in_s.at[me], 32 + off, 32 + off, bits(me, off)).wait_send()


def attend_rows(query, new_kv, cache_kv, cached_len):
    tok, width = query.shape
    piece = cache_kv.shape[1]
    half = lax.axis_index("exp") // 4
    length = lax.dynamic_index_in_dim(cached_len, lax.axis_index("req"), 0, keepdims=False)
    holder = half * 4 + jnp.arange(4, dtype=jnp.int32)[:, None]
    past = holder * piece + jnp.arange(piece, dtype=jnp.int32)[None, :]
    past = jnp.where(past < length, -1, 1 << 20)
    fresh = holder * tok + jnp.arange(tok, dtype=jnp.int32)[None, :]
    lim = jnp.concatenate([past, fresh], 1).reshape(1, -1)
    bf16, f32 = jnp.bfloat16, jnp.float32
    span = width // KVH
    return pl.pallas_call(
        attend_kernel,
        out_shape=jax.ShapeDtypeStruct(query.shape, query.dtype),
        in_specs=[VMEM_SPEC] * 4,
        out_specs=VMEM_SPEC,
        scratch_shapes=[
            pltpu.VMEM((8, tok, span), bf16),
            pltpu.VMEM((4, piece + tok, HD), bf16),
            pltpu.VMEM((4, piece + tok, HD), bf16),
            pltpu.VMEM((7, tok, span), bf16),
            pltpu.VMEM((7, tok, 128), f32),
            pltpu.VMEM((8, tok, span), bf16),
            pltpu.VMEM((8, tok, 128), f32),
            pltpu.SemaphoreType.DMA((5,)),
            pltpu.SemaphoreType.DMA((40,)),
            pltpu.SemaphoreType.DMA((40,)),
        ],
        compiler_params=pltpu.CompilerParams(
            collective_id=3, has_side_effects=True, vmem_limit_bytes=32 * 2**20
        ),
        name="attend_rows",
    )(query, new_kv, cache_kv, lim)


def shards(
    query, new_kv, cache_kv, cached_len, residual, w_out, gain, routes, gates, w_gate, w_up, w_down
):
    tok_rows = query.shape[0]
    n_exp = lax.axis_size("exp")
    n_req = lax.axis_size("req")
    req_here = cache_kv.shape[0]
    piece_len = cache_kv.shape[1]
    kv_cols = cache_kv.shape[2] // 2
    new_len = tok_rows * n_exp // req_here
    group_index = lax.axis_index("req")
    column = lax.axis_index("exp")
    if (n_req, n_exp, tok_rows, req_here, piece_len) == (4, 8, 64, 1, 256):
        attended = attend_rows(query, new_kv, cache_kv, cached_len)
    else:
        lens_group = lax.dynamic_slice_in_dim(cached_len, group_index * req_here, req_here)
        keys_local = jnp.concatenate([cache_kv.reshape(req_here * piece_len, 2 * kv_cols), new_kv], 0)
        block_rows = keys_local.shape[0]
        q_all = lax.all_gather(query, "exp", axis=0, tiled=True)
        count = q_all.shape[0]
        seen = visibility(
            jnp.arange(block_rows, dtype=jnp.int32),
            column,
            jnp.arange(count, dtype=jnp.int32),
            lens_group,
            piece_len,
            tok_rows,
            new_len,
        )
        scores = head_scores(q_all, keys_local[:, :kv_cols])
        masked = jnp.where(seen[:, None, None, :], scores, -1e30)
        peak = jnp.max(masked, axis=-1)
        expo = jnp.where(seen[:, None, None, :], jnp.exp(masked - peak[..., None]), 0.0)
        total = jnp.sum(expo, axis=-1)
        partial_value = weighted_values(expo.astype(jnp.bfloat16), keys_local[:, kv_cols:]).reshape(
            count, H * HD
        )
        peaks, totals, partials = (
            lax.all_to_all(
                peak.reshape(count, H).astype(jnp.bfloat16),
                "exp",
                split_axis=0,
                concat_axis=0,
                tiled=True,
            ).astype(jnp.float32),
            lax.all_to_all(
                total.reshape(count, H).astype(jnp.bfloat16),
                "exp",
                split_axis=0,
                concat_axis=0,
                tiled=True,
            ).astype(jnp.float32),
            lax.all_to_all(
                partial_value.astype(jnp.bfloat16), "exp", split_axis=0, concat_axis=0, tiled=True
            ).astype(partial_value.dtype),
        )
        peaks = peaks.reshape(n_exp, tok_rows, H)
        totals = totals.reshape(n_exp, tok_rows, H)
        top = jnp.max(peaks, axis=0)
        factor = jnp.exp(peaks - top[None])
        denom = jnp.sum(factor * totals, axis=0)
        numer = jnp.sum(factor[..., None] * partials.reshape(n_exp, tok_rows, H, HD), axis=0)
        attended = (numer / denom[..., None]).reshape(tok_rows, H * HD).astype(jnp.bfloat16)
    stream = (
        residual.astype(jnp.float32) + jnp.dot(attended, w_out, preferred_element_type=jnp.float32)
    ).astype(jnp.bfloat16)
    wide = stream.astype(jnp.float32)
    normed = (
        wide * lax.rsqrt(jnp.mean(wide * wide, axis=-1, keepdims=True) + 1e-06) * gain
    ).astype(jnp.bfloat16)
    rows_here = w_gate.shape[0]
    devices = n_req * n_exp
    if (n_req, n_exp, tok_rows, rows_here) == (4, 8, 64, 4):
        return routed(stream, normed, routes, gates, w_gate, w_up, w_down)
    flat = routes.reshape(-1)
    hits = (flat[:, None] == jnp.arange(EXPERTS, dtype=jnp.int32)[None, :]).astype(jnp.int32)
    slot = jnp.sum(hits * (jnp.cumsum(hits, axis=0) - 1), axis=1)
    place = flat * CAP + slot
    width = EXPERTS * CAP
    chosen = (place[:, None] == jnp.arange(width, dtype=jnp.int32)[None, :]).reshape(
        tok_rows, TOPK, width
    )
    sender = jnp.sum(chosen.astype(jnp.float32), axis=1).astype(jnp.bfloat16)
    send = jnp.einsum("tp,td->pd", sender, normed, preferred_element_type=jnp.float32).astype(
        jnp.bfloat16
    )
    send = send.reshape(EXPERTS // rows_here, rows_here * CAP, D)
    spread = jnp.concatenate([send] * HALVES, 0)
    mixer = jnp.sum(jnp.where(chosen, gates.astype(jnp.float32)[:, :, None], 0.0), axis=1).astype(
        jnp.bfloat16
    )
    arrived = lax.all_to_all(spread, ("req", "exp"), split_axis=0, concat_axis=0, tiled=True)
    pieces = arrived.reshape(devices, rows_here, CAP, D)
    gate_v = jnp.einsum("srcd,rdf->srcf", pieces, w_gate, preferred_element_type=jnp.float32)
    up_v = jnp.einsum("srcd,rdf->srcf", pieces, w_up, preferred_element_type=jnp.float32)
    hidden = (jax.nn.silu(gate_v) * up_v).astype(jnp.bfloat16)
    result = jnp.einsum("srcf,rfd->srcd", hidden, w_down, preferred_element_type=jnp.float32)
    partial_out = result.astype(jnp.bfloat16).reshape(devices, rows_here * CAP, D)
    collected = lax.all_to_all(partial_out, ("req", "exp"), split_axis=0, concat_axis=0, tiled=True)
    back = jnp.sum(collected.reshape(HALVES, width, D).astype(jnp.float32), axis=0).astype(
        jnp.bfloat16
    )
    mixed = jnp.dot(mixer, back, preferred_element_type=jnp.float32)
    return (stream.astype(jnp.float32) + mixed).astype(jnp.bfloat16)


def solution(mesh):
    return jax.shard_map(
        shards,
        mesh=mesh,
        in_specs=(
            P(("req", "exp"), None),
            P(("req", "exp"), None),
            P("req", "exp", None),
            P(),
            P(("req", "exp"), None),
            P(),
            P(),
            P(("req", "exp"), None),
            P(("req", "exp"), None),
            P(("req", "exp"), None, None),
            P(("req", "exp"), None, None),
            P(("req", "exp"), None, None),
        ),
        out_specs=P(("req", "exp"), None),
        check_vma=False,
    )
```

```python
import math

import jax
import jax.numpy as jnp
from jax import lax
from jax.experimental import pallas as pl
from jax.experimental.pallas import tpu as pltpu
from jax.sharding import PartitionSpec as P

D = 2048
H = 16
KVH = 4
HD = 128
EXPERTS = 64
TOPK = 6
HALVES = 2
CAP = 7


def visibility(key_row, key_device, query_index, lens_group, piece_len, tok_rows, new_len):
    req_here = lens_group.shape[0]
    cache_rows = req_here * piece_len
    is_cache = key_row < cache_rows
    cache_req = key_row // piece_len
    cache_pos = key_device * piece_len + key_row % piece_len
    new_token = key_device * tok_rows + key_row - cache_rows
    key_req = jnp.where(is_cache, cache_req, new_token // new_len)
    key_pos = new_token % new_len
    owners = jnp.arange(req_here, dtype=jnp.int32)
    cache_len = jnp.sum(
        jnp.where(cache_req[:, None] == owners[None, :], lens_group[None, :], 0), axis=1
    )
    query_req = query_index // new_len
    query_pos = query_index % new_len
    same = key_req[None, :] == query_req[:, None]
    seen = jnp.where(
        is_cache[None, :], (cache_pos < cache_len)[None, :], key_pos[None, :] <= query_pos[:, None]
    )
    return same & seen


def head_scores(queries, keys):
    count = queries.shape[0]
    qh = queries.reshape(count, KVH, H // KVH, HD)
    kh = keys.reshape(keys.shape[0], KVH, HD)
    return jnp.einsum("qgjd,kgd->qgjk", qh, kh, preferred_element_type=jnp.float32) * (
        1.0 / math.sqrt(HD)
    )


def weighted_values(weights, values):
    vh = values.reshape(values.shape[0], KVH, HD)
    return jnp.einsum("qgjk,kgd->qgjd", weights, vh, preferred_element_type=jnp.float32)


MESH = pl.DeviceIdType.MESH
VMEM_SPEC = pl.BlockSpec(memory_space=pltpu.VMEM)
ANY_SPEC = pl.BlockSpec(memory_space=pl.ANY)
OFFSETS = (1, 3, 2)


def place_here():
    row, col = lax.axis_index("req"), lax.axis_index("exp")
    return row // 2, col % 2, col // 2, row % 2


def peer(x, y, z, c):
    return (2 * x + c, 2 * z + y)


def block_of(x, y, z, c):
    return (2 * x + c) * 8 + 2 * z + y


def stepped(x, y, c, da, db):
    dx = jnp.where(c == 0, db, da)
    dy = jnp.where(c == 0, da, db)
    return jnp.bitwise_xor(x, dx), jnp.bitwise_xor(y, dy)


def greet(peers):
    barrier = pltpu.get_barrier_semaphore()
    for other in peers:
        pl.semaphore_signal(barrier, inc=1, device_id=other, device_id_type=MESH)
    pl.semaphore_wait(barrier, len(peers))


def partners(x, y, z, c):
    xa, ya = stepped(x, y, c, 1, 0)
    xb, yb = stepped(x, y, c, 0, 1)
    along = {k: peer(x, y, (z + k) % 4, c) for k in OFFSETS}
    return along, peer(xa, ya, z, c), peer(xb, yb, z, c), peer(x, y, z, 1 - c)


def label(da, db, k):
    return (da * 2 + db) * 4 + k


def gather_kernel(mine_ref, note_ref, out_ref, notes_ref, local_sem, send_sem, recv_sem):
    x, y, z, c = place_here()
    along, a_peer, b_peer, core_peer = partners(x, y, z, c)
    greet([*along.values(), a_peer, b_peer, core_peer])
    sent = []

    def send(src, note, block, slot, target):
        for lane, (one, dst) in enumerate(((note, notes_ref), (src, out_ref))):
            copy = pltpu.make_async_remote_copy(
                src_ref=one,
                dst_ref=dst.at[block],
                send_sem=send_sem.at[len(sent)],
                recv_sem=recv_sem.at[2 * slot + lane],
                device_id=target,
                device_id_type=MESH,
            )
            copy.start()
            sent.append(copy)

    def arrived(block, slot):
        for lane, (one, dst) in enumerate(((note_ref, notes_ref), (mine_ref, out_ref))):
            pltpu.make_async_remote_copy(
                src_ref=one,
                dst_ref=dst.at[block],
                send_sem=send_sem.at[0],
                recv_sem=recv_sem.at[2 * slot + lane],
                device_id=core_peer,
                device_id_type=MESH,
            ).wait_recv()

    def block(da, db, k):
        xs, ys = stepped(x, y, c, da, db)
        return block_of(xs, ys, (z + k) % 4, c)

    own = block_of(x, y, z, c)
    send(mine_ref, note_ref, own, label(0, 1, 0), b_peer)
    send(mine_ref, note_ref, own, label(1, 0, 0), a_peer)
    for k in OFFSETS:
        send(mine_ref, note_ref, own, label(0, 0, (4 - k) % 4), along[k])
    send(mine_ref, note_ref, own, 16 + label(0, 0, 0), core_peer)
    keep = pltpu.make_async_copy(mine_ref, out_ref.at[own], local_sem.at[0])
    keep.start()
    jot = pltpu.make_async_copy(note_ref, notes_ref.at[own], local_sem.at[1])
    jot.start()

    def relay(da, db, k):
        b = block(da, db, k)
        arrived(b, label(da, db, k))
        if db == 0:
            send(out_ref.at[b], notes_ref.at[b], b, label(da, 1, k), b_peer)
            if da == 0:
                send(out_ref.at[b], notes_ref.at[b], b, label(1, 0, k), a_peer)
        send(out_ref.at[b], notes_ref.at[b], b, 16 + label(da, db, k), core_peer)

    relay(1, 0, 0)
    for k in OFFSETS:
        relay(0, 0, k)
    relay(0, 1, 0)
    for k in OFFSETS:
        relay(1, 0, k)
    relay(1, 1, 0)
    for k in OFFSETS:
        relay(0, 1, k)
    for k in OFFSETS:
        relay(1, 1, k)
    for da in range(2):
        for db in range(2):
            for k in range(4):
                xs, ys = stepped(x, y, 1 - c, da, db)
                arrived(block_of(xs, ys, (z + k) % 4, 1 - c), 16 + label(da, db, k))
    keep.wait()
    jot.wait()
    for copy in sent:
        copy.wait_send()


def gather_rows(mine, note):
    whole = lambda one: jax.ShapeDtypeStruct((32, *one.shape), one.dtype)
    return pl.pallas_call(
        gather_kernel,
        out_shape=(whole(mine), whole(note)),
        in_specs=[VMEM_SPEC, VMEM_SPEC],
        out_specs=(ANY_SPEC, ANY_SPEC),
        scratch_shapes=[
            pltpu.SemaphoreType.DMA((2,)),
            pltpu.SemaphoreType.DMA((62,)),
            pltpu.SemaphoreType.DMA((64,)),
        ],
        compiler_params=pltpu.CompilerParams(collective_id=1, has_side_effects=True),
        name="gather_rows",
    )(mine, note)


def reduce_kernel(
    mixer_ref, outs_ref, stream_ref, out_ref, out_c, in_c, in_b, in_a, in_z, sum_c, sum_b, sum_a, send_sem, recv_sem
):
    x, y, z, c = place_here()
    along, a_peer, b_peer, core_peer = partners(x, y, z, c)
    greet([*along.values(), a_peer, b_peer, core_peer])
    sent = []
    f32 = jnp.float32

    def send(src, dst, slot, target):
        copy = pltpu.make_async_remote_copy(
            src_ref=src,
            dst_ref=dst,
            send_sem=send_sem.at[len(sent)],
            recv_sem=recv_sem.at[slot],
            device_id=target,
            device_id_type=MESH,
        )
        copy.start()
        sent.append(copy)

    def arrived(dst, slot):
        pltpu.make_async_remote_copy(
            src_ref=dst,
            dst_ref=dst,
            send_sem=send_sem.at[0],
            recv_sem=recv_sem.at[slot],
            device_id=core_peer,
            device_id_type=MESH,
        ).wait_recv()

    def add(dst, one, two):
        rows = dst.shape[0]

        @pl.loop(0, rows // 16)
        def _(i):
            part = pl.ds(pl.multiple_of(i * 16, 16), 16)
            dst[part, :] = (one[part, :].astype(f32) + two[part, :].astype(f32)).astype(dst.dtype)

    ks = (*OFFSETS, 0)
    order = [(da, db, k) for db in (1, 0) for da in (1, 0) for k in ks]
    def mixed(b):
        return jnp.dot(mixer_ref[b], outs_ref[b // 4], preferred_element_type=f32)

    def give(da, db, k):
        xs, ys = stepped(x, y, 1 - c, da, db)
        i = label(da, db, k)
        out_c[i] = mixed(block_of(xs, ys, (z + k) % 4, 1 - c)).astype(out_c.dtype)
        send(out_c.at[i], in_c.at[i], i, core_peer)

    def take(da, db, k):
        i = label(da, db, k)
        xs, ys = stepped(x, y, c, da, db)
        term = mixed(block_of(xs, ys, (z + k) % 4, c))
        arrived(in_c.at[i], i)
        sum_c[i] = (term + in_c[i].astype(f32)).astype(sum_c.dtype)
        if db == 1:
            send(sum_c.at[i], in_b.at[da * 4 + k], 16 + da * 4 + k, b_peer)

    lag = 2
    for n in range(len(order) + lag):
        if n < len(order):
            give(*order[n])
        if n >= lag:
            take(*order[n - lag])
    for da in (1, 0):
        for k in ks:
            j = da * 4 + k
            arrived(in_b.at[j], 16 + j)
            add(sum_b.at[j], sum_c.at[label(da, 0, k)], in_b.at[j])
            if da == 1:
                send(sum_b.at[j], in_a.at[k], 24 + k, a_peer)
    for k in ks:
        arrived(in_a.at[k], 24 + k)
        add(sum_a.at[k], sum_b.at[k], in_a.at[k])
        if k:
            send(sum_a.at[k], in_z.at[4 - k], 28 + (4 - k), along[k])
    for k in OFFSETS:
        arrived(in_z.at[k], 28 + k)
    rows = out_ref.shape[0]

    @pl.loop(0, rows // 16)
    def _(i):
        part = pl.ds(pl.multiple_of(i * 16, 16), 16)
        whole = sum_a[0, part, :].astype(f32)
        for k in OFFSETS:
            whole += in_z[k, part, :].astype(f32)
        out_ref[part, :] = (stream_ref[part, :].astype(f32) + whole).astype(out_ref.dtype)

    for copy in sent:
        copy.wait_send()


def reduce_rows(mixer, outs, stream):
    rows, width = stream.shape
    space = lambda n: pltpu.VMEM((n, rows, width), jnp.bfloat16)
    return pl.pallas_call(
        reduce_kernel,
        out_shape=jax.ShapeDtypeStruct(stream.shape, stream.dtype),
        in_specs=[VMEM_SPEC] * 3,
        out_specs=VMEM_SPEC,
        scratch_shapes=[
            space(16),
            space(16),
            space(8),
            space(4),
            space(4),
            space(16),
            space(8),
            space(4),
            pltpu.SemaphoreType.DMA((31,)),
            pltpu.SemaphoreType.DMA((32,)),
        ],
        compiler_params=pltpu.CompilerParams(
            collective_id=2, has_side_effects=True, vmem_limit_bytes=48 * 2**20
        ),
        name="reduce_rows",
    )(mixer, outs, stream)


def pick_kernel(all_ref, note_ref, first_ref, rows_ref, mixer_ref):
    lots, tok, width = all_ref.shape
    count = mixer_ref.shape[2]
    here = count // 32
    note = note_ref[...].reshape(lots * tok, 128).astype(jnp.float32)
    first = first_ref[...].astype(jnp.float32)
    lane = lax.broadcasted_iota(jnp.int32, (lots * tok, count), 1).astype(jnp.float32)
    token = lax.broadcasted_iota(jnp.int32, (lots * tok, 1), 0)
    lot = (token // tok).astype(jnp.float32)
    pick = jnp.zeros((lots * tok, count), jnp.float32)
    mixer = pick
    for k in range(TOPK):
        expert = note[:, k : k + 1] - first
        row = expert * 32 + lot * CAP + note[:, TOPK + k : TOPK + k + 1]
        same = lane == jnp.where((expert >= 0) & (expert < here), row, -1.0)
        pick = jnp.where(same, 1.0, pick)
        mixer = jnp.where(same, note[:, 2 * TOPK + k : 2 * TOPK + k + 1], mixer)
    mixer_ref[...] = mixer.astype(mixer_ref.dtype).reshape(lots, tok, count)
    rows = lax.dot_general(
        pick.T.astype(jnp.bfloat16),
        all_ref[...].reshape(lots * tok, width),
        (((1,), (0,)), ((), ())),
        preferred_element_type=jnp.float32,
    )
    rows_ref[...] = rows.astype(rows_ref.dtype).reshape(1, here, 32, width)


def pick_rows(everyone, notes, first, here):
    blocks, tok, width = everyone.shape
    return pl.pallas_call(
        pick_kernel,
        out_shape=(
            jax.ShapeDtypeStruct((blocks // 4, here, 32, width), everyone.dtype),
            jax.ShapeDtypeStruct((blocks, tok, here * 32), everyone.dtype),
        ),
        grid=(blocks // 4,),
        in_specs=[
            pl.BlockSpec((4, tok, width), lambda g: (g, 0, 0)),
            pl.BlockSpec((4, tok, 128), lambda g: (g, 0, 0)),
            pl.BlockSpec((1, 1), lambda g: (0, 0)),
        ],
        out_specs=(
            pl.BlockSpec((1, here, 32, width), lambda g: (g, 0, 0, 0)),
            pl.BlockSpec((4, tok, here * 32), lambda g: (g, 0, 0)),
        ),
        compiler_params=pltpu.CompilerParams(vmem_limit_bytes=24 * 2**20),
        name="pick_rows",
    )(everyone, notes, first)


def expert_kernel(rows_ref, gate_ref, up_ref, down_ref, out_ref):
    groups, _, count, width = rows_ref.shape
    rows = rows_ref[...].reshape(groups * count, width)
    across = (((1,), (1,)), ((), ()))
    gate = lax.dot_general(rows, gate_ref[0], across, preferred_element_type=jnp.float32)
    up = lax.dot_general(rows, up_ref[0], across, preferred_element_type=jnp.float32)
    hidden = (gate / (1.0 + jnp.exp(-gate)) * up).astype(jnp.bfloat16)
    part = jnp.dot(hidden, down_ref[0], preferred_element_type=jnp.float32)
    out_ref[...] = part.astype(jnp.bfloat16).reshape(groups, 1, count, width)


def run_experts(rows, w_gate, w_up, w_down):
    groups, here, count, width = rows.shape
    ff = w_gate.shape[2]
    lot = pl.BlockSpec((groups, 1, count, width), lambda r: (0, r, 0, 0))
    return pl.pallas_call(
        expert_kernel,
        out_shape=jax.ShapeDtypeStruct(rows.shape, rows.dtype),
        grid=(here,),
        in_specs=[
            lot,
            pl.BlockSpec((1, ff, width), lambda r: (r, 0, 0)),
            pl.BlockSpec((1, ff, width), lambda r: (r, 0, 0)),
            pl.BlockSpec((1, ff, width), lambda r: (r, 0, 0)),
        ],
        out_specs=lot,
        compiler_params=pltpu.CompilerParams(vmem_limit_bytes=48 * 2**20),
        name="run_experts",
    )(rows, w_gate.swapaxes(1, 2), w_up.swapaxes(1, 2), w_down)


def routed(stream, normed, routes, gates, w_gate, w_up, w_down):
    tok_rows = stream.shape[0]
    rows_here = w_gate.shape[0]
    me = lax.axis_index("req") * lax.axis_size("exp") + lax.axis_index("exp")
    flat = routes.reshape(-1)
    hits = (flat[:, None] == jnp.arange(EXPERTS, dtype=jnp.int32)[None, :]).astype(jnp.int32)
    slot = jnp.sum(hits * (jnp.cumsum(hits, axis=0) - 1), axis=1)
    note = jnp.concatenate(
        [routes.astype(gates.dtype), slot.reshape(tok_rows, TOPK).astype(gates.dtype), gates], 1
    )
    note = jnp.pad(note, ((0, 0), (0, 128 - 3 * TOPK)))
    everyone, notes = gather_rows(normed, note)
    first = (me * rows_here % EXPERTS).reshape(1, 1)
    rows, mixer = pick_rows(everyone, notes, first, rows_here)
    outs = run_experts(rows, w_gate, w_up, w_down).reshape(8, rows_here * 32, D)
    return reduce_rows(mixer, outs, stream)


def attend_kernel(
    q_ref, new_ref, cache_ref, lim_ref, out_ref,
    q_all, keys, values, out_n, out_s, in_n, in_s, local_sem, send_sem, recv_sem,
):
    row, me = lax.axis_index("req"), lax.axis_index("exp")
    f32 = jnp.float32
    bits = jnp.bitwise_xor
    greet([(row, bits(me, off)) for off in range(1, 8)])
    tok, fresh = q_ref.shape[0], cache_ref.shape[1]
    span = q_ref.shape[1] // KVH
    kv_cols = KVH * HD

    def pieces(head):
        at = lambda first: pl.ds(pl.multiple_of(first + head * HD, HD), HD)
        lot = me % 4
        old, new = pl.ds(0, fresh), pl.ds(fresh, tok)
        return (
            (cache_ref.at[0, :, at(0)], keys.at[lot, old, :]),
            (new_ref.at[:, at(0)], keys.at[lot, new, :]),
            (cache_ref.at[0, :, at(kv_cols)], values.at[lot, old, :]),
            (new_ref.at[:, at(kv_cols)], values.at[lot, new, :]),
        )

    def remote(src, dst, out_slot, in_slot, target):
        return pltpu.make_async_remote_copy(
            src_ref=src,
            dst_ref=dst,
            send_sem=send_sem.at[out_slot],
            recv_sem=recv_sem.at[in_slot],
            device_id=(row, target),
            device_id_type=MESH,
        )

    def q_piece(head):
        return q_ref.at[:, pl.ds(pl.multiple_of(head * span, span), span)]

    sent, local = [], []
    for off in (3, 2, 1):
        other = bits(me, off)
        for i, (src, dst) in enumerate(pieces(other % 4)):
            n = 8 + off * 4 + i
            sent.append(remote(src, dst, n, n, other))
            sent[-1].start()
    for off in (7, 6, 5, 4, 3, 2, 1):
        other = bits(me, off)
        sent.append(remote(q_piece(other % 4), q_all.at[me], off, off, other))
        sent[-1].start()
    for i, (src, dst) in enumerate((*pieces(me % 4), (q_piece(me % 4), q_all.at[me]))):
        local.append(pltpu.make_async_copy(src, dst, local_sem.at[i]))
        local[-1].start()
    for copy in local:
        copy.wait()
    for off in (1, 2, 3):
        lot = bits(me, off) % 4
        old, new = pl.ds(0, fresh), pl.ds(fresh, tok)
        lands = (keys.at[lot, old, :], keys.at[lot, new, :], values.at[lot, old, :], values.at[lot, new, :])
        for i, dst in enumerate(lands):
            n = 8 + off * 4 + i
            remote(dst, dst, n, n, bits(me, off)).wait_recv()

    def attend(owner):
        q = q_all[owner]
        group = H // KVH
        stacked = jnp.concatenate([q[:, h * HD : (h + 1) * HD] for h in range(group)], 0)
        k = keys[...].reshape(-1, HD)
        v = values[...].reshape(-1, HD)
        across = (((1,), (1,)), ((), ()))
        scores = lax.dot_general(stacked, k, across, preferred_element_type=f32)
        scores = scores * (1.0 / math.sqrt(HD))
        here = owner * tok + lax.broadcasted_iota(jnp.int32, (group * tok, 1), 0) % tok
        seen = lim_ref[...] <= here
        masked = jnp.where(seen, scores, -1e30)
        peak = jnp.max(masked, axis=1, keepdims=True)
        expo = jnp.where(seen, jnp.exp(masked - peak), 0.0)
        total = jnp.sum(expo, axis=1, keepdims=True)
        numer = jnp.dot(expo.astype(jnp.bfloat16), v, preferred_element_type=f32)
        lane = lax.broadcasted_iota(jnp.int32, (tok, 128), 1)
        stats = jnp.zeros((tok, 128), f32)
        parts = []
        for h in range(group):
            rows = slice(h * tok, (h + 1) * tok)
            stats = jnp.where(lane == h, peak[rows], stats)
            stats = jnp.where(lane == group + h, total[rows], stats)
            parts.append(numer[rows])
        return jnp.concatenate(parts, 1).astype(jnp.bfloat16), stats

    @pl.loop(0, 7)
    def _(step):
        off = 7 - step
        owner = bits(me, off)
        remote(q_all.at[owner], q_all.at[owner], off, off, owner).wait_recv()
        numer, stats = attend(owner)
        out_n[step] = numer
        out_s[step] = stats
        remote(out_n.at[step], in_n.at[me], 24 + off, 24 + off, owner).start()
        remote(out_s.at[step], in_s.at[me], 32 + off, 32 + off, owner).start()

    numer, stats = attend(me)
    in_n[me] = numer
    in_s[me] = stats
    for off in range(1, 8):
        other = bits(me, off)
        remote(in_n.at[other], in_n.at[other], 24 + off, 24 + off, other).wait_recv()
        remote(in_s.at[other], in_s.at[other], 32 + off, 32 + off, other).wait_recv()
    group = H // KVH
    for head in range(KVH):
        one, two = in_s[head], in_s[KVH + head]
        for h in range(group):
            p1, p2 = one[:, h : h + 1], two[:, h : h + 1]
            top = jnp.maximum(p1, p2)
            f1, f2 = jnp.exp(p1 - top), jnp.exp(p2 - top)
            denom = f1 * one[:, group + h : group + h + 1] + f2 * two[:, group + h : group + h + 1]
            cols = slice(h * HD, (h + 1) * HD)
            numer = f1 * in_n[head, :, cols].astype(f32) + f2 * in_n[KVH + head, :, cols].astype(f32)
            at = (head * group + h) * HD
            out_ref[:, at : at + HD] = (numer / denom).astype(out_ref.dtype)
    for copy in sent:
        copy.wait_send()
    for off in range(1, 8):
        remote(out_n.at[7 - off], in_n.at[me], 24 + off, 24 + off, bits(me, off)).wait_send()
        remote(out_s.at[7 - off], in_s.at[me], 32 + off, 32 + off, bits(me, off)).wait_send()


def attend_rows(query, new_kv, cache_kv, cached_len):
    tok, width = query.shape
    piece = cache_kv.shape[1]
    half = lax.axis_index("exp") // 4
    length = lax.dynamic_index_in_dim(cached_len, lax.axis_index("req"), 0, keepdims=False)
    holder = half * 4 + jnp.arange(4, dtype=jnp.int32)[:, None]
    past = holder * piece + jnp.arange(piece, dtype=jnp.int32)[None, :]
    past = jnp.where(past < length, -1, 1 << 20)
    fresh = holder * tok + jnp.arange(tok, dtype=jnp.int32)[None, :]
    lim = jnp.concatenate([past, fresh], 1).reshape(1, -1)
    bf16, f32 = jnp.bfloat16, jnp.float32
    span = width // KVH
    return pl.pallas_call(
        attend_kernel,
        out_shape=jax.ShapeDtypeStruct(query.shape, query.dtype),
        in_specs=[VMEM_SPEC] * 4,
        out_specs=VMEM_SPEC,
        scratch_shapes=[
            pltpu.VMEM((8, tok, span), bf16),
            pltpu.VMEM((4, piece + tok, HD), bf16),
            pltpu.VMEM((4, piece + tok, HD), bf16),
            pltpu.VMEM((7, tok, span), bf16),
            pltpu.VMEM((7, tok, 128), f32),
            pltpu.VMEM((8, tok, span), bf16),
            pltpu.VMEM((8, tok, 128), f32),
            pltpu.SemaphoreType.DMA((5,)),
            pltpu.SemaphoreType.DMA((40,)),
            pltpu.SemaphoreType.DMA((40,)),
        ],
        compiler_params=pltpu.CompilerParams(
            collective_id=3, has_side_effects=True, vmem_limit_bytes=32 * 2**20
        ),
        name="attend_rows",
    )(query, new_kv, cache_kv, lim)


def shards(
    query, new_kv, cache_kv, cached_len, residual, w_out, gain, routes, gates, w_gate, w_up, w_down
):
    tok_rows = query.shape[0]
    n_exp = lax.axis_size("exp")
    n_req = lax.axis_size("req")
    req_here = cache_kv.shape[0]
    piece_len = cache_kv.shape[1]
    kv_cols = cache_kv.shape[2] // 2
    new_len = tok_rows * n_exp // req_here
    group_index = lax.axis_index("req")
    column = lax.axis_index("exp")
    if (n_req, n_exp, tok_rows, req_here, piece_len) == (4, 8, 64, 1, 256):
        attended = attend_rows(query, new_kv, cache_kv, cached_len)
    else:
        lens_group = lax.dynamic_slice_in_dim(cached_len, group_index * req_here, req_here)
        keys_local = jnp.concatenate([cache_kv.reshape(req_here * piece_len, 2 * kv_cols), new_kv], 0)
        block_rows = keys_local.shape[0]
        q_all = lax.all_gather(query, "exp", axis=0, tiled=True)
        count = q_all.shape[0]
        seen = visibility(
            jnp.arange(block_rows, dtype=jnp.int32),
            column,
            jnp.arange(count, dtype=jnp.int32),
            lens_group,
            piece_len,
            tok_rows,
            new_len,
        )
        scores = head_scores(q_all, keys_local[:, :kv_cols])
        masked = jnp.where(seen[:, None, None, :], scores, -1e30)
        peak = jnp.max(masked, axis=-1)
        expo = jnp.where(seen[:, None, None, :], jnp.exp(masked - peak[..., None]), 0.0)
        total = jnp.sum(expo, axis=-1)
        partial_value = weighted_values(expo.astype(jnp.bfloat16), keys_local[:, kv_cols:]).reshape(
            count, H * HD
        )
        peaks, totals, partials = (
            lax.all_to_all(
                peak.reshape(count, H).astype(jnp.bfloat16),
                "exp",
                split_axis=0,
                concat_axis=0,
                tiled=True,
            ).astype(jnp.float32),
            lax.all_to_all(
                total.reshape(count, H).astype(jnp.bfloat16),
                "exp",
                split_axis=0,
                concat_axis=0,
                tiled=True,
            ).astype(jnp.float32),
            lax.all_to_all(
                partial_value.astype(jnp.bfloat16), "exp", split_axis=0, concat_axis=0, tiled=True
            ).astype(partial_value.dtype),
        )
        peaks = peaks.reshape(n_exp, tok_rows, H)
        totals = totals.reshape(n_exp, tok_rows, H)
        top = jnp.max(peaks, axis=0)
        factor = jnp.exp(peaks - top[None])
        denom = jnp.sum(factor * totals, axis=0)
        numer = jnp.sum(factor[..., None] * partials.reshape(n_exp, tok_rows, H, HD), axis=0)
        attended = (numer / denom[..., None]).reshape(tok_rows, H * HD).astype(jnp.bfloat16)
    stream = (
        residual.astype(jnp.float32) + jnp.dot(attended, w_out, preferred_element_type=jnp.float32)
    ).astype(jnp.bfloat16)
    wide = stream.astype(jnp.float32)
    normed = (
        wide * lax.rsqrt(jnp.mean(wide * wide, axis=-1, keepdims=True) + 1e-06) * gain
    ).astype(jnp.bfloat16)
    rows_here = w_gate.shape[0]
    devices = n_req * n_exp
    if (n_req, n_exp, tok_rows, rows_here) == (4, 8, 64, 4):
        return routed(stream, normed, routes, gates, w_gate, w_up, w_down)
    flat = routes.reshape(-1)
    hits = (flat[:, None] == jnp.arange(EXPERTS, dtype=jnp.int32)[None, :]).astype(jnp.int32)
    slot = jnp.sum(hits * (jnp.cumsum(hits, axis=0) - 1), axis=1)
    place = flat * CAP + slot
    width = EXPERTS * CAP
    chosen = (place[:, None] == jnp.arange(width, dtype=jnp.int32)[None, :]).reshape(
        tok_rows, TOPK, width
    )
    sender = jnp.sum(chosen.astype(jnp.float32), axis=1).astype(jnp.bfloat16)
    send = jnp.einsum("tp,td->pd", sender, normed, preferred_element_type=jnp.float32).astype(
        jnp.bfloat16
    )
    send = send.reshape(EXPERTS // rows_here, rows_here * CAP, D)
    spread = jnp.concatenate([send] * HALVES, 0)
    mixer = jnp.sum(jnp.where(chosen, gates.astype(jnp.float32)[:, :, None], 0.0), axis=1).astype(
        jnp.bfloat16
    )
    arrived = lax.all_to_all(spread, ("req", "exp"), split_axis=0, concat_axis=0, tiled=True)
    pieces = arrived.reshape(devices, rows_here, CAP, D)
    gate_v = jnp.einsum("srcd,rdf->srcf", pieces, w_gate, preferred_element_type=jnp.float32)
    up_v = jnp.einsum("srcd,rdf->srcf", pieces, w_up, preferred_element_type=jnp.float32)
    hidden = (jax.nn.silu(gate_v) * up_v).astype(jnp.bfloat16)
    result = jnp.einsum("srcf,rfd->srcd", hidden, w_down, preferred_element_type=jnp.float32)
    partial_out = result.astype(jnp.bfloat16).reshape(devices, rows_here * CAP, D)
    collected = lax.all_to_all(partial_out, ("req", "exp"), split_axis=0, concat_axis=0, tiled=True)
    back = jnp.sum(collected.reshape(HALVES, width, D).astype(jnp.float32), axis=0).astype(
        jnp.bfloat16
    )
    mixed = jnp.dot(mixer, back, preferred_element_type=jnp.float32)
    return (stream.astype(jnp.float32) + mixed).astype(jnp.bfloat16)


def solution(mesh):
    return jax.shard_map(
        shards,
        mesh=mesh,
        in_specs=(
            P(("req", "exp"), None),
            P(("req", "exp"), None),
            P("req", "exp", None),
            P(),
            P(("req", "exp"), None),
            P(),
            P(),
            P(("req", "exp"), None),
            P(("req", "exp"), None),
            P(("req", "exp"), None, None),
            P(("req", "exp"), None, None),
            P(("req", "exp"), None, None),
        ),
        out_specs=P(("req", "exp"), None),
        check_vma=False,
    )
```

```python
import math

import jax
import jax.numpy as jnp
from jax import lax
from jax.experimental import pallas as pl
from jax.experimental.pallas import tpu as pltpu
from jax.sharding import PartitionSpec as P

D = 2048
H = 16
KVH = 4
HD = 128
EXPERTS = 64
TOPK = 6
HALVES = 2
CAP = 7


def visibility(key_row, key_device, query_index, lens_group, piece_len, tok_rows, new_len):
    req_here = lens_group.shape[0]
    cache_rows = req_here * piece_len
    is_cache = key_row < cache_rows
    cache_req = key_row // piece_len
    cache_pos = key_device * piece_len + key_row % piece_len
    new_token = key_device * tok_rows + key_row - cache_rows
    key_req = jnp.where(is_cache, cache_req, new_token // new_len)
    key_pos = new_token % new_len
    owners = jnp.arange(req_here, dtype=jnp.int32)
    cache_len = jnp.sum(
        jnp.where(cache_req[:, None] == owners[None, :], lens_group[None, :], 0), axis=1
    )
    query_req = query_index // new_len
    query_pos = query_index % new_len
    same = key_req[None, :] == query_req[:, None]
    seen = jnp.where(
        is_cache[None, :], (cache_pos < cache_len)[None, :], key_pos[None, :] <= query_pos[:, None]
    )
    return same & seen


def head_scores(queries, keys):
    count = queries.shape[0]
    qh = queries.reshape(count, KVH, H // KVH, HD)
    kh = keys.reshape(keys.shape[0], KVH, HD)
    return jnp.einsum("qgjd,kgd->qgjk", qh, kh, preferred_element_type=jnp.float32) * (
        1.0 / math.sqrt(HD)
    )


def weighted_values(weights, values):
    vh = values.reshape(values.shape[0], KVH, HD)
    return jnp.einsum("qgjk,kgd->qgjd", weights, vh, preferred_element_type=jnp.float32)


MESH = pl.DeviceIdType.MESH
VMEM_SPEC = pl.BlockSpec(memory_space=pltpu.VMEM)
ANY_SPEC = pl.BlockSpec(memory_space=pl.ANY)
OFFSETS = (2, 1, 3)


def place_here():
    row, col = lax.axis_index("req"), lax.axis_index("exp")
    return row // 2, col % 2, col // 2, row % 2


def peer(x, y, z, c):
    return (2 * x + c, 2 * z + y)


def block_of(x, y, z, c):
    return (2 * x + c) * 8 + 2 * z + y


def stepped(x, y, c, da, db):
    dx = jnp.where(c == 0, db, da)
    dy = jnp.where(c == 0, da, db)
    return jnp.bitwise_xor(x, dx), jnp.bitwise_xor(y, dy)


def greet(peers):
    barrier = pltpu.get_barrier_semaphore()
    for other in peers:
        pl.semaphore_signal(barrier, inc=1, device_id=other, device_id_type=MESH)
    pl.semaphore_wait(barrier, len(peers))


def partners(x, y, z, c):
    xa, ya = stepped(x, y, c, 1, 0)
    xb, yb = stepped(x, y, c, 0, 1)
    along = {k: peer(x, y, (z + k) % 4, c) for k in OFFSETS}
    return along, peer(xa, ya, z, c), peer(xb, yb, z, c), peer(x, y, z, 1 - c)


def label(da, db, k):
    return (da * 2 + db) * 4 + k


def gather_kernel(mine_ref, note_ref, out_ref, notes_ref, local_sem, send_sem, recv_sem):
    x, y, z, c = place_here()
    along, a_peer, b_peer, core_peer = partners(x, y, z, c)
    greet([*along.values(), a_peer, b_peer, core_peer])
    sent = []

    def send(src, note, block, slot, target):
        for lane, (one, dst) in enumerate(((note, notes_ref), (src, out_ref))):
            copy = pltpu.make_async_remote_copy(
                src_ref=one,
                dst_ref=dst.at[block],
                send_sem=send_sem.at[len(sent)],
                recv_sem=recv_sem.at[2 * slot + lane],
                device_id=target,
                device_id_type=MESH,
            )
            copy.start()
            sent.append(copy)

    def arrived(block, slot):
        for lane, (one, dst) in enumerate(((note_ref, notes_ref), (mine_ref, out_ref))):
            pltpu.make_async_remote_copy(
                src_ref=one,
                dst_ref=dst.at[block],
                send_sem=send_sem.at[0],
                recv_sem=recv_sem.at[2 * slot + lane],
                device_id=core_peer,
                device_id_type=MESH,
            ).wait_recv()

    def block(da, db, k):
        xs, ys = stepped(x, y, c, da, db)
        return block_of(xs, ys, (z + k) % 4, c)

    own = block_of(x, y, z, c)
    send(mine_ref, note_ref, own, label(0, 1, 0), b_peer)
    send(mine_ref, note_ref, own, label(1, 0, 0), a_peer)
    for k in OFFSETS:
        send(mine_ref, note_ref, own, label(0, 0, (4 - k) % 4), along[k])
    send(mine_ref, note_ref, own, 16 + label(0, 0, 0), core_peer)
    keep = pltpu.make_async_copy(mine_ref, out_ref.at[own], local_sem.at[0])
    keep.start()
    jot = pltpu.make_async_copy(note_ref, notes_ref.at[own], local_sem.at[1])
    jot.start()

    def relay(da, db, k):
        b = block(da, db, k)
        arrived(b, label(da, db, k))
        if db == 0:
            send(out_ref.at[b], notes_ref.at[b], b, label(da, 1, k), b_peer)
            if da == 0:
                send(out_ref.at[b], notes_ref.at[b], b, label(1, 0, k), a_peer)
        send(out_ref.at[b], notes_ref.at[b], b, 16 + label(da, db, k), core_peer)

    relay(1, 0, 0)
    for k in OFFSETS:
        relay(0, 0, k)
    relay(0, 1, 0)
    for k in OFFSETS:
        relay(1, 0, k)
    relay(1, 1, 0)
    for k in OFFSETS:
        relay(0, 1, k)
    for k in OFFSETS:
        relay(1, 1, k)
    for da in range(2):
        for db in range(2):
            for k in range(4):
                xs, ys = stepped(x, y, 1 - c, da, db)
                arrived(block_of(xs, ys, (z + k) % 4, 1 - c), 16 + label(da, db, k))
    keep.wait()
    jot.wait()
    for copy in sent:
        copy.wait_send()


def gather_rows(mine, note):
    whole = lambda one: jax.ShapeDtypeStruct((32, *one.shape), one.dtype)
    return pl.pallas_call(
        gather_kernel,
        out_shape=(whole(mine), whole(note)),
        in_specs=[VMEM_SPEC, VMEM_SPEC],
        out_specs=(ANY_SPEC, ANY_SPEC),
        scratch_shapes=[
            pltpu.SemaphoreType.DMA((2,)),
            pltpu.SemaphoreType.DMA((62,)),
            pltpu.SemaphoreType.DMA((64,)),
        ],
        compiler_params=pltpu.CompilerParams(collective_id=1, has_side_effects=True),
        name="gather_rows",
    )(mine, note)


def reduce_kernel(
    mixer_ref, outs_ref, stream_ref, out_ref, out_c, in_c, in_b, in_a, in_z, sum_c, sum_b, sum_a, send_sem, recv_sem
):
    x, y, z, c = place_here()
    along, a_peer, b_peer, core_peer = partners(x, y, z, c)
    greet([*along.values(), a_peer, b_peer, core_peer])
    sent = []
    f32 = jnp.float32

    def send(src, dst, slot, target):
        copy = pltpu.make_async_remote_copy(
            src_ref=src,
            dst_ref=dst,
            send_sem=send_sem.at[len(sent)],
            recv_sem=recv_sem.at[slot],
            device_id=target,
            device_id_type=MESH,
        )
        copy.start()
        sent.append(copy)

    def arrived(dst, slot):
        pltpu.make_async_remote_copy(
            src_ref=dst,
            dst_ref=dst,
            send_sem=send_sem.at[0],
            recv_sem=recv_sem.at[slot],
            device_id=core_peer,
            device_id_type=MESH,
        ).wait_recv()

    def add(dst, one, two):
        rows = dst.shape[0]

        @pl.loop(0, rows // 16)
        def _(i):
            part = pl.ds(pl.multiple_of(i * 16, 16), 16)
            dst[part, :] = (one[part, :].astype(f32) + two[part, :].astype(f32)).astype(dst.dtype)

    ks = (*OFFSETS, 0)
    order = [(da, db, k) for db in (1, 0) for da in (1, 0) for k in ks]
    def mixed(b):
        return jnp.dot(mixer_ref[b], outs_ref[b // 4], preferred_element_type=f32)

    def give(da, db, k):
        xs, ys = stepped(x, y, 1 - c, da, db)
        i = label(da, db, k)
        out_c[i] = mixed(block_of(xs, ys, (z + k) % 4, 1 - c)).astype(out_c.dtype)
        send(out_c.at[i], in_c.at[i], i, core_peer)

    def take(da, db, k):
        i = label(da, db, k)
        xs, ys = stepped(x, y, c, da, db)
        term = mixed(block_of(xs, ys, (z + k) % 4, c))
        arrived(in_c.at[i], i)
        sum_c[i] = (term + in_c[i].astype(f32)).astype(sum_c.dtype)
        if db == 1:
            send(sum_c.at[i], in_b.at[da * 4 + k], 16 + da * 4 + k, b_peer)

    lag = 1
    for n in range(len(order) + lag):
        if n < len(order):
            give(*order[n])
        if n >= lag:
            take(*order[n - lag])
    for da in (1, 0):
        for k in ks:
            j = da * 4 + k
            arrived(in_b.at[j], 16 + j)
            add(sum_b.at[j], sum_c.at[label(da, 0, k)], in_b.at[j])
            if da == 1:
                send(sum_b.at[j], in_a.at[k], 24 + k, a_peer)
    for k in ks:
        arrived(in_a.at[k], 24 + k)
        add(sum_a.at[k], sum_b.at[k], in_a.at[k])
        if k:
            send(sum_a.at[k], in_z.at[4 - k], 28 + (4 - k), along[k])
    for k in OFFSETS:
        arrived(in_z.at[k], 28 + k)
    rows = out_ref.shape[0]

    @pl.loop(0, rows // 16)
    def _(i):
        part = pl.ds(pl.multiple_of(i * 16, 16), 16)
        whole = sum_a[0, part, :].astype(f32)
        for k in OFFSETS:
            whole += in_z[k, part, :].astype(f32)
        out_ref[part, :] = (stream_ref[part, :].astype(f32) + whole).astype(out_ref.dtype)

    for copy in sent:
        copy.wait_send()


def reduce_rows(mixer, outs, stream):
    rows, width = stream.shape
    space = lambda n: pltpu.VMEM((n, rows, width), jnp.bfloat16)
    return pl.pallas_call(
        reduce_kernel,
        out_shape=jax.ShapeDtypeStruct(stream.shape, stream.dtype),
        in_specs=[VMEM_SPEC] * 3,
        out_specs=VMEM_SPEC,
        scratch_shapes=[
            space(16),
            space(16),
            space(8),
            space(4),
            space(4),
            space(16),
            space(8),
            space(4),
            pltpu.SemaphoreType.DMA((31,)),
            pltpu.SemaphoreType.DMA((32,)),
        ],
        compiler_params=pltpu.CompilerParams(
            collective_id=2, has_side_effects=True, vmem_limit_bytes=48 * 2**20
        ),
        name="reduce_rows",
    )(mixer, outs, stream)


def pick_kernel(all_ref, note_ref, first_ref, rows_ref, mixer_ref):
    lots, tok, width = all_ref.shape
    count = mixer_ref.shape[2]
    here = count // 32
    note = note_ref[...].reshape(lots * tok, 128).astype(jnp.float32)
    first = first_ref[...].astype(jnp.float32)
    lane = lax.broadcasted_iota(jnp.int32, (lots * tok, count), 1).astype(jnp.float32)
    token = lax.broadcasted_iota(jnp.int32, (lots * tok, 1), 0)
    lot = (token // tok).astype(jnp.float32)
    pick = jnp.zeros((lots * tok, count), jnp.float32)
    mixer = pick
    for k in range(TOPK):
        expert = note[:, k : k + 1] - first
        row = expert * 32 + lot * CAP + note[:, TOPK + k : TOPK + k + 1]
        same = lane == jnp.where((expert >= 0) & (expert < here), row, -1.0)
        pick = jnp.where(same, 1.0, pick)
        mixer = jnp.where(same, note[:, 2 * TOPK + k : 2 * TOPK + k + 1], mixer)
    mixer_ref[...] = mixer.astype(mixer_ref.dtype).reshape(lots, tok, count)
    rows = lax.dot_general(
        pick.T.astype(jnp.bfloat16),
        all_ref[...].reshape(lots * tok, width),
        (((1,), (0,)), ((), ())),
        preferred_element_type=jnp.float32,
    )
    rows_ref[...] = rows.astype(rows_ref.dtype).reshape(1, here, 32, width)


def pick_rows(everyone, notes, first, here):
    blocks, tok, width = everyone.shape
    return pl.pallas_call(
        pick_kernel,
        out_shape=(
            jax.ShapeDtypeStruct((blocks // 4, here, 32, width), everyone.dtype),
            jax.ShapeDtypeStruct((blocks, tok, here * 32), everyone.dtype),
        ),
        grid=(blocks // 4,),
        in_specs=[
            pl.BlockSpec((4, tok, width), lambda g: (g, 0, 0)),
            pl.BlockSpec((4, tok, 128), lambda g: (g, 0, 0)),
            pl.BlockSpec((1, 1), lambda g: (0, 0)),
        ],
        out_specs=(
            pl.BlockSpec((1, here, 32, width), lambda g: (g, 0, 0, 0)),
            pl.BlockSpec((4, tok, here * 32), lambda g: (g, 0, 0)),
        ),
        compiler_params=pltpu.CompilerParams(vmem_limit_bytes=24 * 2**20),
        name="pick_rows",
    )(everyone, notes, first)


def expert_kernel(rows_ref, gate_ref, up_ref, down_ref, out_ref):
    groups, _, count, width = rows_ref.shape
    rows = rows_ref[...].reshape(groups * count, width)
    across = (((1,), (1,)), ((), ()))
    gate = lax.dot_general(rows, gate_ref[0], across, preferred_element_type=jnp.float32)
    up = lax.dot_general(rows, up_ref[0], across, preferred_element_type=jnp.float32)
    hidden = (gate / (1.0 + jnp.exp(-gate)) * up).astype(jnp.bfloat16)
    part = jnp.dot(hidden, down_ref[0], preferred_element_type=jnp.float32)
    out_ref[...] = part.astype(jnp.bfloat16).reshape(groups, 1, count, width)


def run_experts(rows, w_gate, w_up, w_down):
    groups, here, count, width = rows.shape
    ff = w_gate.shape[2]
    lot = pl.BlockSpec((groups, 1, count, width), lambda r: (0, r, 0, 0))
    return pl.pallas_call(
        expert_kernel,
        out_shape=jax.ShapeDtypeStruct(rows.shape, rows.dtype),
        grid=(here,),
        in_specs=[
            lot,
            pl.BlockSpec((1, ff, width), lambda r: (r, 0, 0)),
            pl.BlockSpec((1, ff, width), lambda r: (r, 0, 0)),
            pl.BlockSpec((1, ff, width), lambda r: (r, 0, 0)),
        ],
        out_specs=lot,
        compiler_params=pltpu.CompilerParams(vmem_limit_bytes=48 * 2**20),
        name="run_experts",
    )(rows, w_gate.swapaxes(1, 2), w_up.swapaxes(1, 2), w_down)


def routed(stream, normed, routes, gates, w_gate, w_up, w_down):
    tok_rows = stream.shape[0]
    rows_here = w_gate.shape[0]
    me = lax.axis_index("req") * lax.axis_size("exp") + lax.axis_index("exp")
    flat = routes.reshape(-1)
    hits = (flat[:, None] == jnp.arange(EXPERTS, dtype=jnp.int32)[None, :]).astype(jnp.int32)
    slot = jnp.sum(hits * (jnp.cumsum(hits, axis=0) - 1), axis=1)
    note = jnp.concatenate(
        [routes.astype(gates.dtype), slot.reshape(tok_rows, TOPK).astype(gates.dtype), gates], 1
    )
    note = jnp.pad(note, ((0, 0), (0, 128 - 3 * TOPK)))
    everyone, notes = gather_rows(normed, note)
    first = (me * rows_here % EXPERTS).reshape(1, 1)
    rows, mixer = pick_rows(everyone, notes, first, rows_here)
    outs = run_experts(rows, w_gate, w_up, w_down).reshape(8, rows_here * 32, D)
    return reduce_rows(mixer, outs, stream)


def attend_kernel(
    q_ref, new_ref, cache_ref, lim_ref, out_ref,
    q_all, keys, values, out_n, out_s, in_n, in_s, local_sem, send_sem, recv_sem,
):
    row, me = lax.axis_index("req"), lax.axis_index("exp")
    f32 = jnp.float32
    bits = jnp.bitwise_xor
    greet([(row, bits(me, off)) for off in range(1, 8)])
    tok, fresh = q_ref.shape[0], cache_ref.shape[1]
    span = q_ref.shape[1] // KVH
    kv_cols = KVH * HD

    def pieces(head):
        at = lambda first: pl.ds(pl.multiple_of(first + head * HD, HD), HD)
        lot = me % 4
        old, new = pl.ds(0, fresh), pl.ds(fresh, tok)
        return (
            (cache_ref.at[0, :, at(0)], keys.at[lot, old, :]),
            (new_ref.at[:, at(0)], keys.at[lot, new, :]),
            (cache_ref.at[0, :, at(kv_cols)], values.at[lot, old, :]),
            (new_ref.at[:, at(kv_cols)], values.at[lot, new, :]),
        )

    def remote(src, dst, out_slot, in_slot, target):
        return pltpu.make_async_remote_copy(
            src_ref=src,
            dst_ref=dst,
            send_sem=send_sem.at[out_slot],
            recv_sem=recv_sem.at[in_slot],
            device_id=(row, target),
            device_id_type=MESH,
        )

    def q_piece(head):
        return q_ref.at[:, pl.ds(pl.multiple_of(head * span, span), span)]

    sent, local = [], []
    for off in (3, 2, 1):
        other = bits(me, off)
        for i, (src, dst) in enumerate(pieces(other % 4)):
            n = 8 + off * 4 + i
            sent.append(remote(src, dst, n, n, other))
            sent[-1].start()
    for off in (7, 6, 5, 4, 3, 2, 1):
        other = bits(me, off)
        sent.append(remote(q_piece(other % 4), q_all.at[me], off, off, other))
        sent[-1].start()
    for i, (src, dst) in enumerate((*pieces(me % 4), (q_piece(me % 4), q_all.at[me]))):
        local.append(pltpu.make_async_copy(src, dst, local_sem.at[i]))
        local[-1].start()
    for copy in local:
        copy.wait()
    for off in (1, 2, 3):
        lot = bits(me, off) % 4
        old, new = pl.ds(0, fresh), pl.ds(fresh, tok)
        lands = (keys.at[lot, old, :], keys.at[lot, new, :], values.at[lot, old, :], values.at[lot, new, :])
        for i, dst in enumerate(lands):
            n = 8 + off * 4 + i
            remote(dst, dst, n, n, bits(me, off)).wait_recv()

    def attend(owner):
        q = q_all[owner]
        group = H // KVH
        stacked = jnp.concatenate([q[:, h * HD : (h + 1) * HD] for h in range(group)], 0)
        k = keys[...].reshape(-1, HD)
        v = values[...].reshape(-1, HD)
        across = (((1,), (1,)), ((), ()))
        scores = lax.dot_general(stacked, k, across, preferred_element_type=f32)
        scores = scores * (1.0 / math.sqrt(HD))
        here = owner * tok + lax.broadcasted_iota(jnp.int32, (group * tok, 1), 0) % tok
        seen = lim_ref[...] <= here
        masked = jnp.where(seen, scores, -1e30)
        peak = jnp.max(masked, axis=1, keepdims=True)
        expo = jnp.where(seen, jnp.exp(masked - peak), 0.0)
        total = jnp.sum(expo, axis=1, keepdims=True)
        numer = jnp.dot(expo.astype(jnp.bfloat16), v, preferred_element_type=f32)
        lane = lax.broadcasted_iota(jnp.int32, (tok, 128), 1)
        stats = jnp.zeros((tok, 128), f32)
        parts = []
        for h in range(group):
            rows = slice(h * tok, (h + 1) * tok)
            stats = jnp.where(lane == h, peak[rows], stats)
            stats = jnp.where(lane == group + h, total[rows], stats)
            parts.append(numer[rows])
        return jnp.concatenate(parts, 1).astype(jnp.bfloat16), stats

    @pl.loop(0, 7)
    def _(step):
        off = 7 - step
        owner = bits(me, off)
        remote(q_all.at[owner], q_all.at[owner], off, off, owner).wait_recv()
        numer, stats = attend(owner)
        out_n[step] = numer
        out_s[step] = stats
        remote(out_n.at[step], in_n.at[me], 24 + off, 24 + off, owner).start()
        remote(out_s.at[step], in_s.at[me], 32 + off, 32 + off, owner).start()

    numer, stats = attend(me)
    in_n[me] = numer
    in_s[me] = stats
    for off in range(1, 8):
        other = bits(me, off)
        remote(in_n.at[other], in_n.at[other], 24 + off, 24 + off, other).wait_recv()
        remote(in_s.at[other], in_s.at[other], 32 + off, 32 + off, other).wait_recv()
    group = H // KVH
    for head in range(KVH):
        one, two = in_s[head], in_s[KVH + head]
        for h in range(group):
            p1, p2 = one[:, h : h + 1], two[:, h : h + 1]
            top = jnp.maximum(p1, p2)
            f1, f2 = jnp.exp(p1 - top), jnp.exp(p2 - top)
            denom = f1 * one[:, group + h : group + h + 1] + f2 * two[:, group + h : group + h + 1]
            cols = slice(h * HD, (h + 1) * HD)
            numer = f1 * in_n[head, :, cols].astype(f32) + f2 * in_n[KVH + head, :, cols].astype(f32)
            at = (head * group + h) * HD
            out_ref[:, at : at + HD] = (numer / denom).astype(out_ref.dtype)
    for copy in sent:
        copy.wait_send()
    for off in range(1, 8):
        remote(out_n.at[7 - off], in_n.at[me], 24 + off, 24 + off, bits(me, off)).wait_send()
        remote(out_s.at[7 - off], in_s.at[me], 32 + off, 32 + off, bits(me, off)).wait_send()


def attend_rows(query, new_kv, cache_kv, cached_len):
    tok, width = query.shape
    piece = cache_kv.shape[1]
    half = lax.axis_index("exp") // 4
    length = lax.dynamic_index_in_dim(cached_len, lax.axis_index("req"), 0, keepdims=False)
    holder = half * 4 + jnp.arange(4, dtype=jnp.int32)[:, None]
    past = holder * piece + jnp.arange(piece, dtype=jnp.int32)[None, :]
    past = jnp.where(past < length, -1, 1 << 20)
    fresh = holder * tok + jnp.arange(tok, dtype=jnp.int32)[None, :]
    lim = jnp.concatenate([past, fresh], 1).reshape(1, -1)
    bf16, f32 = jnp.bfloat16, jnp.float32
    span = width // KVH
    return pl.pallas_call(
        attend_kernel,
        out_shape=jax.ShapeDtypeStruct(query.shape, query.dtype),
        in_specs=[VMEM_SPEC] * 4,
        out_specs=VMEM_SPEC,
        scratch_shapes=[
            pltpu.VMEM((8, tok, span), bf16),
            pltpu.VMEM((4, piece + tok, HD), bf16),
            pltpu.VMEM((4, piece + tok, HD), bf16),
            pltpu.VMEM((7, tok, span), bf16),
            pltpu.VMEM((7, tok, 128), f32),
            pltpu.VMEM((8, tok, span), bf16),
            pltpu.VMEM((8, tok, 128), f32),
            pltpu.SemaphoreType.DMA((5,)),
            pltpu.SemaphoreType.DMA((40,)),
            pltpu.SemaphoreType.DMA((40,)),
        ],
        compiler_params=pltpu.CompilerParams(
            collective_id=3, has_side_effects=True, vmem_limit_bytes=32 * 2**20
        ),
        name="attend_rows",
    )(query, new_kv, cache_kv, lim)


def shards(
    query, new_kv, cache_kv, cached_len, residual, w_out, gain, routes, gates, w_gate, w_up, w_down
):
    tok_rows = query.shape[0]
    n_exp = lax.axis_size("exp")
    n_req = lax.axis_size("req")
    req_here = cache_kv.shape[0]
    piece_len = cache_kv.shape[1]
    kv_cols = cache_kv.shape[2] // 2
    new_len = tok_rows * n_exp // req_here
    group_index = lax.axis_index("req")
    column = lax.axis_index("exp")
    if (n_req, n_exp, tok_rows, req_here, piece_len) == (4, 8, 64, 1, 256):
        attended = attend_rows(query, new_kv, cache_kv, cached_len)
    else:
        lens_group = lax.dynamic_slice_in_dim(cached_len, group_index * req_here, req_here)
        keys_local = jnp.concatenate([cache_kv.reshape(req_here * piece_len, 2 * kv_cols), new_kv], 0)
        block_rows = keys_local.shape[0]
        q_all = lax.all_gather(query, "exp", axis=0, tiled=True)
        count = q_all.shape[0]
        seen = visibility(
            jnp.arange(block_rows, dtype=jnp.int32),
            column,
            jnp.arange(count, dtype=jnp.int32),
            lens_group,
            piece_len,
            tok_rows,
            new_len,
        )
        scores = head_scores(q_all, keys_local[:, :kv_cols])
        masked = jnp.where(seen[:, None, None, :], scores, -1e30)
        peak = jnp.max(masked, axis=-1)
        expo = jnp.where(seen[:, None, None, :], jnp.exp(masked - peak[..., None]), 0.0)
        total = jnp.sum(expo, axis=-1)
        partial_value = weighted_values(expo.astype(jnp.bfloat16), keys_local[:, kv_cols:]).reshape(
            count, H * HD
        )
        peaks, totals, partials = (
            lax.all_to_all(
                peak.reshape(count, H).astype(jnp.bfloat16),
                "exp",
                split_axis=0,
                concat_axis=0,
                tiled=True,
            ).astype(jnp.float32),
            lax.all_to_all(
                total.reshape(count, H).astype(jnp.bfloat16),
                "exp",
                split_axis=0,
                concat_axis=0,
                tiled=True,
            ).astype(jnp.float32),
            lax.all_to_all(
                partial_value.astype(jnp.bfloat16), "exp", split_axis=0, concat_axis=0, tiled=True
            ).astype(partial_value.dtype),
        )
        peaks = peaks.reshape(n_exp, tok_rows, H)
        totals = totals.reshape(n_exp, tok_rows, H)
        top = jnp.max(peaks, axis=0)
        factor = jnp.exp(peaks - top[None])
        denom = jnp.sum(factor * totals, axis=0)
        numer = jnp.sum(factor[..., None] * partials.reshape(n_exp, tok_rows, H, HD), axis=0)
        attended = (numer / denom[..., None]).reshape(tok_rows, H * HD).astype(jnp.bfloat16)
    stream = (
        residual.astype(jnp.float32) + jnp.dot(attended, w_out, preferred_element_type=jnp.float32)
    ).astype(jnp.bfloat16)
    wide = stream.astype(jnp.float32)
    normed = (
        wide * lax.rsqrt(jnp.mean(wide * wide, axis=-1, keepdims=True) + 1e-06) * gain
    ).astype(jnp.bfloat16)
    rows_here = w_gate.shape[0]
    devices = n_req * n_exp
    if (n_req, n_exp, tok_rows, rows_here) == (4, 8, 64, 4):
        return routed(stream, normed, routes, gates, w_gate, w_up, w_down)
    flat = routes.reshape(-1)
    hits = (flat[:, None] == jnp.arange(EXPERTS, dtype=jnp.int32)[None, :]).astype(jnp.int32)
    slot = jnp.sum(hits * (jnp.cumsum(hits, axis=0) - 1), axis=1)
    place = flat * CAP + slot
    width = EXPERTS * CAP
    chosen = (place[:, None] == jnp.arange(width, dtype=jnp.int32)[None, :]).reshape(
        tok_rows, TOPK, width
    )
    sender = jnp.sum(chosen.astype(jnp.float32), axis=1).astype(jnp.bfloat16)
    send = jnp.einsum("tp,td->pd", sender, normed, preferred_element_type=jnp.float32).astype(
        jnp.bfloat16
    )
    send = send.reshape(EXPERTS // rows_here, rows_here * CAP, D)
    spread = jnp.concatenate([send] * HALVES, 0)
    mixer = jnp.sum(jnp.where(chosen, gates.astype(jnp.float32)[:, :, None], 0.0), axis=1).astype(
        jnp.bfloat16
    )
    arrived = lax.all_to_all(spread, ("req", "exp"), split_axis=0, concat_axis=0, tiled=True)
    pieces = arrived.reshape(devices, rows_here, CAP, D)
    gate_v = jnp.einsum("srcd,rdf->srcf", pieces, w_gate, preferred_element_type=jnp.float32)
    up_v = jnp.einsum("srcd,rdf->srcf", pieces, w_up, preferred_element_type=jnp.float32)
    hidden = (jax.nn.silu(gate_v) * up_v).astype(jnp.bfloat16)
    result = jnp.einsum("srcf,rfd->srcd", hidden, w_down, preferred_element_type=jnp.float32)
    partial_out = result.astype(jnp.bfloat16).reshape(devices, rows_here * CAP, D)
    collected = lax.all_to_all(partial_out, ("req", "exp"), split_axis=0, concat_axis=0, tiled=True)
    back = jnp.sum(collected.reshape(HALVES, width, D).astype(jnp.float32), axis=0).astype(
        jnp.bfloat16
    )
    mixed = jnp.dot(mixer, back, preferred_element_type=jnp.float32)
    return (stream.astype(jnp.float32) + mixed).astype(jnp.bfloat16)


def solution(mesh):
    return jax.shard_map(
        shards,
        mesh=mesh,
        in_specs=(
            P(("req", "exp"), None),
            P(("req", "exp"), None),
            P("req", "exp", None),
            P(),
            P(("req", "exp"), None),
            P(),
            P(),
            P(("req", "exp"), None),
            P(("req", "exp"), None),
            P(("req", "exp"), None, None),
            P(("req", "exp"), None, None),
            P(("req", "exp"), None, None),
        ),
        out_specs=P(("req", "exp"), None),
        check_vma=False,
    )
```
